128 devices in a mesh: facet: 8 (over y, core), sub: 16 (over z, x).
Axes of the slice: x: 4, y: 4, z: 4, core: 2. Of those that a mesh axis runs over, the one named last changes fastest.
Arguments:
- facet_data: bfloat16 [2, 16, 65536], P(None, None, ('facet', 'sub')), may hold values from -6 to 6
- subgrid_pos: int32 [128], P(('facet', 'sub')), may hold values from 0 to 65408, as said below
- vis_counts: int32 [128], P(('facet', 'sub')), may hold values from 128 to 512, as said below
- vis_u_fine: int32 [128, 512], P(('facet', 'sub')), may hold values from 0 to 8079
- vis_v_fine: int32 [128, 512], P(('facet', 'sub')), may hold values from 0 to 143
- vis_observed: float32 [2, 128, 512], P(None, ('facet', 'sub')), may hold values from -6 to 6
Outputs:
- vis_residual: float32 [2, 128, 512], P(None, ('facet', 'sub'))
- facet_residual: float32 [2, 16, 65536], P(None, None, ('facet', 'sub'))
The draws below stay inside these ranges and needn't reach their ends.
Inputs may be any that keep to these rules, and one draw needn't show every extreme that they name: `subgrid_pos`: distinct multiples of 128; a subgrid's u cells o to o + 511 are taken modulo 65536. The first vis_counts[s] slots of subgrid s are live; some subgrid has all 512 slots live.
All inputs are finite; a program needn't handle non-finite values.
Results may differ from the reference program's by a relative error of at most 0.012.
Values may be sent and summed in bfloat16 or wider, within the bound.
No kernel may reach another device: no remote copies, remote signals or barrier semaphores. Data moves between devices by JAX's collectives and lax.ppermute only.
A program may use at most 64 MiB of HBM per device.

```python
import math
import jax
import jax.numpy as jnp
from jax import lax

SG = 512
KS = 8
OVER = 16
VR = 16
VIS = 512
NX = 65536
S_TOTAL = 128


def slot_product(left_side, right_side):
    right_high = right_side // 256
    right_low = right_side % 256
    return (left_side * right_low % NX + left_side * right_high % NX * 256) % NX


def special_spot(key):
    spot_count = 4 * NX // SG
    chosen_spot = jax.random.randint(jax.random.fold_in(key, 7), (), 5, spot_count - 5).astype(jnp.int32)
    below_cells = jax.random.randint(jax.random.fold_in(key, 8), (), SG // 16, 3 * SG // 16 + 1).astype(jnp.int32)
    return (chosen_spot, below_cells)


def draw_subgrid_pos(key, part):
    spot_count = 4 * NX // SG
    chosen_spot, below_cells = special_spot(key)
    spot_ids = jnp.arange(spot_count, dtype=jnp.int32)
    ranking = jax.random.permutation(jax.random.fold_in(key, 11), spot_count).astype(jnp.int32)
    excluded = (spot_ids == 0) | (spot_ids == spot_count - 1) | (spot_ids >= chosen_spot - 4) & (spot_ids <= chosen_spot)
    ranking = jnp.where(excluded, ranking + spot_count, ranking)
    ordered = jnp.argsort(ranking, stable=True).astype(jnp.int32)
    others = ordered[:S_TOTAL - 3]
    fixed_spots = jnp.stack([jnp.int32(0), jnp.int32(spot_count - 1), chosen_spot]).astype(jnp.int32)
    all_spots = jnp.concatenate([fixed_spots, others])
    shuffle = jax.random.permutation(jax.random.fold_in(key, 12), S_TOTAL)
    return (all_spots[shuffle] * (SG // 4)).astype(jnp.int32)


def draw_vis_counts(key, part):
    key_first, key_second = jax.random.split(key)
    counts = jax.random.randint(key_first, (S_TOTAL,), VIS // 4, VIS + 1).astype(jnp.int32)
    full_spot = jax.random.randint(key_second, (), 0, S_TOTAL)
    return counts.at[full_spot].set(VIS).astype(jnp.int32)


def draw_facet_data(key, part):
    chosen_spot, below_cells = special_spot(key)
    tone_cell = chosen_spot * (SG // 4) - below_cells
    column_ids = jnp.arange(NX, dtype=jnp.int32)
    tone_index = slot_product(column_ids, tone_cell)
    tone_angle = 2.0 * math.pi * (tone_index.astype(jnp.float32) / float(NX))
    row_angle = jax.random.uniform(jax.random.fold_in(key, 21), (VR, 1), jnp.float32, -math.pi, math.pi)
    total_angle = tone_angle[None, :] + row_angle
    tone_part = 4.0 * jnp.stack([jnp.cos(total_angle), jnp.sin(total_angle)])
    noise_part = 0.5 * jax.random.normal(jax.random.fold_in(key, 22), (2, VR, NX), jnp.float32)
    return jnp.clip(tone_part + noise_part, -6.0, 6.0).astype(jnp.bfloat16)


def place_ends(result, own_key, least, top_value):
    shape = result.shape
    spot = [jax.random.randint(jax.random.fold_in(own_key, axis), (), 0, shape[axis]) for axis in range(len(shape))]
    result = result.at[tuple(spot)].set(least)
    longest = shape.index(max(shape))
    spot[longest] = (spot[longest] + 1) % shape[longest]
    return result.at[tuple(spot)].set(top_value)


def level_of(stream_key, dims, cuts, least, largest):
    level = 1.0
    for axis_at, parts in cuts:
        draws = jax.random.uniform(jax.random.fold_in(jax.random.fold_in(stream_key, 6), axis_at), (parts,), jnp.float32, least / len(cuts), largest / len(cuts))
        level = level * jnp.repeat(jnp.exp(draws), dims[axis_at] // parts).reshape((-1,) + (1,) * (len(dims) - 1 - axis_at))
    return level


def noise(rng, dims, scale, reach, cuts=(), kind=jnp.bfloat16):
    values = jax.random.normal(rng, dims, jnp.float32) * scale
    if len(cuts) > 0:
        values = level_of(rng, dims, cuts, -0.22, 0.18) * values
    return jnp.clip(values, min=-reach, max=reach).astype(kind)


def setup_inputs(seed: int = 0) -> dict:
    key_of = jax.random.split(jax.random.key(seed), 7)
    facet_data = draw_facet_data(jax.random.fold_in(key_of[6], 71), 0)
    subgrid_pos = draw_subgrid_pos(jax.random.fold_in(key_of[6], 71), 0)
    vis_counts = draw_vis_counts(jax.random.fold_in(key_of[6], 71), 0)
    vis_u_fine = place_ends(jax.random.randint(key_of[3], (S_TOTAL, VIS), 0, (SG - KS + 1) * OVER), jax.random.fold_in(key_of[3], 1), 0, ((SG - KS + 1) * OVER) - 1).astype(jnp.int32)
    vis_v_fine = place_ends(jax.random.randint(key_of[4], (S_TOTAL, VIS), 0, (VR - KS + 1) * OVER), jax.random.fold_in(key_of[4], 1), 0, ((VR - KS + 1) * OVER) - 1).astype(jnp.int32)
    vis_observed = noise(key_of[5], (2, S_TOTAL, VIS), 1.0, 6.0, ((1, 128),), jnp.float32)
    return {"facet_data": facet_data, "subgrid_pos": subgrid_pos, "vis_counts": vis_counts, "vis_u_fine": vis_u_fine, "vis_v_fine": vis_v_fine, "vis_observed": vis_observed}


def phase_slot_index(left_side, right_side, image_width):
    right_high = right_side // 256
    right_low = right_side % 256
    return (left_side * right_low % image_width + left_side * right_high % image_width * 256) % image_width

def phasor(phase_total_count, image_width):
    phase_angle = 2.0 * math.pi * (phase_total_count.astype(jnp.float32) / float(image_width))
    return (jnp.cos(phase_angle), jnp.sin(phase_angle))

def build_phase_tables(sub_width, image_width):
    table_range = jnp.arange(sub_width, dtype=jnp.int32)
    cosine, sine_part = phasor(phase_slot_index(table_range[:, None], table_range[None, :], image_width), image_width)
    norm_scale = 1.0 / math.sqrt(image_width)
    real_part = (cosine * norm_scale).astype(jnp.bfloat16)
    imag_part = (-sine_part * norm_scale).astype(jnp.bfloat16)
    forward_table = jnp.concatenate([jnp.concatenate([real_part, imag_part], 1), jnp.concatenate([-imag_part, real_part], 1)], 0)
    backward_table = jnp.concatenate([jnp.concatenate([real_part, -imag_part], 1), jnp.concatenate([imag_part, real_part], 1)], 0)
    return (forward_table, backward_table)

def forward_part(columns, x_start, positions, table, image_width):
    sub_width = table.shape[0] // 2
    rows_v = columns.shape[1]
    blocks = columns.shape[2] // sub_width
    inside = jnp.arange(sub_width, dtype=jnp.int32)
    mod_cos, mod_sin = phasor(phase_slot_index(inside[None, :], positions[:, None], image_width), image_width)
    mod_cos = mod_cos[:, None, None, :]
    mod_sin = mod_sin[:, None, None, :]
    image_band = columns.astype(jnp.float32).reshape(2, rows_v, blocks, sub_width)
    real_z = image_band[0][None] * mod_cos + image_band[1][None] * mod_sin
    imag_z = image_band[1][None] * mod_cos - image_band[0][None] * mod_sin
    stacked = jnp.concatenate([real_z, imag_z], -1).astype(jnp.bfloat16)
    partial_grid = jnp.dot(stacked.astype(jnp.float32), table.astype(jnp.float32), precision=lax.Precision.HIGHEST)
    anchors = x_start + jnp.arange(blocks, dtype=jnp.int32) * sub_width
    columns_u = (positions[:, None] + inside[None, :]) % image_width
    post_cos, post_sin = phasor(phase_slot_index(anchors[None, :, None], columns_u[:, None, :], image_width), image_width)
    post_cos = post_cos[:, None]
    post_sin = post_sin[:, None]
    real_p = partial_grid[..., :sub_width]
    imag_p = partial_grid[..., sub_width:]
    real_g = lax.optimization_barrier(jnp.sum(real_p * post_cos + imag_p * post_sin, axis=2))
    imag_g = lax.optimization_barrier(jnp.sum(imag_p * post_cos - real_p * post_sin, axis=2))
    return jnp.concatenate([real_g, imag_g], -1)

def kernel_weights(fine_index, cells):
    cell_index = fine_index // OVER
    frac_index = fine_index % OVER
    cell_range = jnp.arange(cells, dtype=jnp.int32)
    cell_offset = cell_range[None, None, :] - cell_index[..., None]
    distance = cell_offset.astype(jnp.float32) - (KS - 1) / 2.0 - frac_index.astype(jnp.float32)[..., None] / OVER
    weight = jnp.exp(-0.5 * (distance / 0.6) ** 2)
    return jnp.where((cell_offset >= 0) & (cell_offset < KS), weight, jnp.float32(0.0))

def degrid_regrid(subgrid_data, u_fine, v_fine, counts, observed):
    sub_width = subgrid_data.shape[2] // 2
    weight_u = kernel_weights(u_fine, sub_width)
    kernel_weight_v = kernel_weights(v_fine, subgrid_data.shape[1])
    gridded_values = subgrid_data.astype(jnp.float32)
    along_v_axis = jnp.einsum('jtz,jzh->jth', kernel_weight_v, gridded_values, precision=lax.Precision.HIGHEST)
    real_pred = lax.optimization_barrier(jnp.sum(along_v_axis[..., :sub_width] * weight_u, -1))
    imag_pred = lax.optimization_barrier(jnp.sum(along_v_axis[..., sub_width:] * weight_u, -1))
    slot_range = jnp.arange(u_fine.shape[1], dtype=jnp.int32)
    live_mask = slot_range[None, :] < counts[:, None]
    real_res = jnp.where(live_mask, observed[0] - real_pred, jnp.float32(0.0))
    imag_res = jnp.where(live_mask, observed[1] - imag_pred, jnp.float32(0.0))
    spread_onto_grid = jnp.concatenate([real_res[..., None] * weight_u, imag_res[..., None] * weight_u], -1)
    regridded_values = jnp.einsum('mlz,mlr->mzr', kernel_weight_v, spread_onto_grid, precision=lax.Precision.HIGHEST).astype(jnp.bfloat16)
    return (jnp.stack([real_res, imag_res]), regridded_values)

def backward_part(grids, positions, x_start, span, table, image_width):
    sub_width = table.shape[0] // 2
    rows_v = grids.shape[1]
    blocks = span // sub_width
    inside = jnp.arange(sub_width, dtype=jnp.int32)
    anchors = x_start + jnp.arange(blocks, dtype=jnp.int32) * sub_width
    columns_u = (positions[:, None] + inside[None, :]) % image_width
    pre_cos, pre_sin = phasor(phase_slot_index(anchors[None, :, None], columns_u[:, None, :], image_width), image_width)
    pre_cos = pre_cos[:, None]
    pre_sin = pre_sin[:, None]
    real_h = grids[..., :sub_width].astype(jnp.float32)[:, :, None, :]
    imag_h = grids[..., sub_width:].astype(jnp.float32)[:, :, None, :]
    real_m = real_h * pre_cos - imag_h * pre_sin
    imag_m = real_h * pre_sin + imag_h * pre_cos
    stacked = jnp.concatenate([real_m, imag_m], -1).astype(jnp.bfloat16)
    product = jnp.dot(stacked.astype(jnp.float32), table.astype(jnp.float32), precision=lax.Precision.HIGHEST)
    mod_cos, mod_sin = phasor(phase_slot_index(inside[None, :], positions[:, None], image_width), image_width)
    mod_cos = mod_cos[:, None, None, :]
    mod_sin = mod_sin[:, None, None, :]
    real_q = product[..., :sub_width]
    imag_q = product[..., sub_width:]
    real_out = lax.optimization_barrier(jnp.sum(real_q * mod_cos - imag_q * mod_sin, axis=0))
    imag_out = lax.optimization_barrier(jnp.sum(real_q * mod_sin + imag_q * mod_cos, axis=0))
    return jnp.stack([real_out, imag_out]).reshape(2, rows_v, span)

def reference(facet_data, subgrid_pos, vis_counts, vis_u_fine, vis_v_fine, vis_observed):
    image_width = NX
    forward_table, backward_table = build_phase_tables(SG, image_width)
    observed = jnp.moveaxis(vis_observed, 1, 0)

    def one_subgrid(carried, sub_items):
        position, amount, u_fine, v_fine, seen_vis = sub_items
        subgrid_data = forward_part(facet_data, 0, position[None], forward_table, image_width).astype(jnp.bfloat16)
        residual, regridded_values = degrid_regrid(subgrid_data, u_fine[None], v_fine[None], amount[None], seen_vis[:, None])
        carried = carried + backward_part(regridded_values, position[None], 0, image_width, backward_table, image_width)
        return (carried, residual[:, 0])
    zero_image = jnp.zeros((2, VR, NX), jnp.float32)
    running, residuals = lax.scan(one_subgrid, zero_image, (subgrid_pos, vis_counts, vis_u_fine, vis_v_fine, observed))
    return (jnp.moveaxis(residuals, 0, 1), running)
```

```python
import math

import jax
import jax.numpy as jnp
import numpy as np
from jax import lax
from jax.sharding import PartitionSpec as P

SG = 512
KS = 8
OVER = 16
RES = 128
BF = jnp.bfloat16
F32 = jnp.float32


def split(value):
    high = lax.reduce_precision(value, 8, 7)
    return high.astype(BF), (value - high).astype(BF)


def complex_rows(cos_part, sin_part):
    return jnp.concatenate(
        [
            jnp.concatenate([cos_part, sin_part], 1),
            jnp.concatenate([-sin_part, cos_part], 1),
        ],
        0,
    )


def gather_by_exchange(value, axis):
    count = lax.axis_size(axis)
    copies = jnp.broadcast_to(value[None], (count,) + value.shape)
    return lax.all_to_all(copies, axis, 0, 0, tiled=True)


def angle_table(rows, columns, period):
    turn = (rows[:, None] * columns[None, :]) % period
    angle = turn.astype(F32) * (2.0 * math.pi / period)
    return jnp.cos(angle), jnp.sin(angle)


def weights(fine_index, cells):
    cell = fine_index // OVER
    frac = fine_index % OVER
    offset = jnp.arange(cells, dtype=jnp.int32)[None, :, None] - cell[:, None, :]
    distance = offset.astype(F32) - (KS - 1) / 2.0 - frac.astype(F32)[:, None, :] / OVER
    weight = jnp.exp(-0.5 * (distance / 0.6) ** 2)
    return jnp.where((offset >= 0) & (offset < KS), weight, F32(0.0))


def shards(facet_data, subgrid_pos, vis_counts, vis_u_fine, vis_v_fine, vis_observed):
    facets = lax.axis_size("facet")
    subs = lax.axis_size("sub")
    rows_v = facet_data.shape[1]
    slots = vis_u_fine.shape[1]
    facet = lax.axis_index("facet")
    inside = jnp.arange(SG, dtype=jnp.int32)
    residue = jnp.arange(RES, dtype=jnp.int32)

    gathered = gather_by_exchange(facet_data, "sub")

    ends = jnp.concatenate([subgrid_pos // RES, vis_counts]).astype(F32)
    meta = jnp.stack(
        [
            vis_u_fine[0].astype(F32),
            vis_v_fine[0].astype(F32),
            vis_observed[0, 0],
            vis_observed[1, 0],
            jnp.pad(ends, (0, slots - 2)),
        ]
    )
    meta = gather_by_exchange(meta, "facet")
    u_fine = meta[:, 0].astype(jnp.int32)
    v_fine = meta[:, 1].astype(jnp.int32)
    observed = meta[:, 2:4]
    spot = meta[:, 4, 0].astype(jnp.int32)
    counts = meta[:, 4, 1].astype(jnp.int32)

    weight_u = weights(u_fine, SG).astype(BF)
    weight_v = weights(v_fine, rows_v)

    blocks = facet * subs + jnp.arange(subs, dtype=jnp.int32)
    cos_d, sin_d = angle_table(residue, blocks, RES)
    high_d, low_d = split(complex_rows(cos_d, sin_d))
    turn = (residue[:, None] * inside[None, :]).astype(F32) * (2.0 * math.pi / 65536)
    tw_cos, tw_sin = jnp.cos(turn)[:, None, :], jnp.sin(turn)[:, None, :]
    lines = (spot[:, None] + jnp.arange(4, dtype=jnp.int32)[None, :]).reshape(-1)
    cos_e, sin_e = angle_table(lines, inside, SG)
    high_e, low_e = split(complex_rows(cos_e, sin_e) * F32(1.0 / 256.0))

    stack = jnp.moveaxis(gathered, 1, 0).reshape(2 * subs, rows_v, SG)
    spread = jnp.einsum("aj,jvx->avx", high_d, stack, preferred_element_type=F32)
    spread = spread + jnp.einsum("aj,jvx->avx", low_d, stack, preferred_element_type=F32)
    real_g, imag_g = spread[:RES], spread[RES:]
    real_h = (real_g * tw_cos + imag_g * tw_sin).astype(BF)
    imag_h = (imag_g * tw_cos - real_g * tw_sin).astype(BF)
    both = jnp.concatenate([real_h, imag_h], -1)
    share = jnp.einsum("rx,fvx->rvf", high_e, both, preferred_element_type=F32)
    share = share + jnp.einsum("rx,fvx->rvf", low_e, both, preferred_element_type=F32)
    share = share.reshape(2, facets, 4, rows_v, RES).transpose(1, 0, 3, 2, 4)
    share = share.reshape(facets, 2, rows_v, SG).astype(BF)
    along = jnp.einsum("scvu,suk->scvk", share, weight_u, preferred_element_type=F32)
    part = jnp.sum(along * weight_v[:, None], 2)

    predicted = jnp.sum(gather_by_exchange(part, "facet"), 0)

    live = inside[None, None, :slots] < counts[:, None, None]
    residual = jnp.where(live, observed - predicted, F32(0.0))
    mine = lax.dynamic_index_in_dim(residual, facet, 0, keepdims=False)[:, None]

    spreaded = (residual[:, :, None] * weight_v[:, None]).astype(BF)
    regrid = jnp.einsum("scvk,suk->scvu", spreaded, weight_u, preferred_element_type=F32)
    regrid = regrid.astype(BF).reshape(facets, 2, rows_v, 4, RES)
    regrid = regrid.transpose(1, 0, 3, 2, 4).reshape(8 * facets, rows_v, RES)
    back = jnp.einsum("rx,rvf->fvx", high_e, regrid, preferred_element_type=F32)
    back = back + jnp.einsum("rx,rvf->fvx", low_e, regrid, preferred_element_type=F32)
    real_b, imag_b = back[..., :SG], back[..., SG:]
    real_m = (real_b * tw_cos - imag_b * tw_sin).astype(BF)
    imag_m = (imag_b * tw_cos + real_b * tw_sin).astype(BF)
    stacked = jnp.concatenate([real_m, imag_m], 0)
    image = jnp.einsum("aj,avx->jvx", high_d, stacked, preferred_element_type=F32)
    image = image + jnp.einsum("aj,avx->jvx", low_d, stacked, preferred_element_type=F32)
    image = image.reshape(2, subs, rows_v, SG).transpose(1, 0, 2, 3).astype(BF)
    image = lax.all_to_all(image, "sub", 0, 0, tiled=True)
    return (mine, jnp.sum(image.astype(F32), 0))


def solution(mesh):
    return jax.shard_map(
        shards,
        mesh=mesh,
        in_specs=(
            P(None, None, ("facet", "sub")),
            P(("facet", "sub")),
            P(("facet", "sub")),
            P(("facet", "sub"), None),
            P(("facet", "sub"), None),
            P(None, ("facet", "sub"), None),
        ),
        out_specs=(P(None, ("facet", "sub"), None), P(None, None, ("facet", "sub"))),
        check_vma=False,
    )
```

```python
import math

import jax
import jax.numpy as jnp
import numpy as np
from jax import lax
from jax.experimental import pallas as pl
from jax.experimental.pallas import tpu as pltpu
from jax.sharding import PartitionSpec as P

SG = 512
KS = 8
OVER = 16
RES = 128
KB = SG // RES
ROWS = 8
BF = jnp.bfloat16
F32 = jnp.float32


def split(value):
    high = lax.reduce_precision(value, 8, 7)
    return high.astype(BF), (value - high).astype(BF)


def gather_by_exchange(value, axis):
    count = lax.axis_size(axis)
    copies = jnp.broadcast_to(value[None], (count,) + value.shape)
    return lax.all_to_all(copies, axis, 0, 0, tiled=True)


def block_tables(facets, subs):
    block = np.arange(facets * subs).reshape(facets, subs)
    turn = (np.arange(RES)[None, :, None] * block[:, None, :]) % RES
    angle = turn * (2.0 * math.pi / RES)
    cos, sin = np.cos(angle), np.sin(angle)
    top = np.stack([cos, sin], -1)
    low = np.stack([-sin, cos], -1)
    table = np.concatenate([top, low], 1).reshape(facets, 2 * RES, 2 * subs)
    return table.astype(np.float32)


def host_split(table):
    high = table.astype(jnp.bfloat16)
    return high, (table - high.astype(np.float32)).astype(jnp.bfloat16)


def weights(fine_index, cells):
    middle = fine_index / OVER + (KS - 1) / 2.0
    cell = jnp.floor(fine_index / OVER)
    row = lax.broadcasted_iota(jnp.int32, (cells, fine_index.shape[1]), 0).astype(F32)
    distance = (row - middle) / 0.6
    weight = jnp.exp(-0.5 * (distance * distance))
    return jnp.where((row >= cell) & (row < cell + KS), weight, F32(0.0))


def dot(left, right, dims):
    return lax.dot_general(left, right, (dims, ((), ())), preferred_element_type=F32)


def forward_kernel(at_ref, y_ref, d_ref, tc_ref, ts_ref, e_ref, *refs):
    groups = (len(refs) - 3) // 2
    meta_refs, wu_refs = refs[:groups], refs[groups : 2 * groups]
    part_ref, ys_ref, gs_ref = refs[2 * groups :]
    pieces = y_ref.shape[0]
    half = e_ref.shape[0] // 2
    band = half // KB
    rows_v = gs_ref.shape[1] // band
    lines = pieces // rows_v
    for k in range(KB):
        ys_ref[k] = y_ref[:, k * RES : (k + 1) * RES].astype(F32)
    for v in range(rows_v):
        row = [ys_ref[k, pl.ds(v, lines, stride=rows_v), :] for k in range(KB)]
        row = jnp.concatenate(row, 1).astype(BF)
        spread = dot(d_ref[...], jnp.concatenate([row, row], 0), ((1,), (0,)))
        real_g, imag_g = spread[:RES], spread[RES:]
        cos, sin = tc_ref[...], ts_ref[...]
        real_h = (real_g * cos + imag_g * sin).astype(BF)
        imag_h = (imag_g * cos - real_g * sin).astype(BF)
        share = dot(e_ref[...], jnp.concatenate([real_h, imag_h], 1), ((1,), (1,)))
        share = share[:half] + share[half:]
        for k in range(KB):
            gs_ref[k, pl.ds(v, band, stride=rows_v), :] = share[k * band : (k + 1) * band]
    for s in range(groups):
        grid = [gs_ref[k, s * 2 * rows_v : (s + 1) * 2 * rows_v, :] for k in range(KB)]
        grid = jnp.concatenate(grid, 1)
        high = grid.astype(BF)
        low = (grid - high.astype(F32)).astype(BF)
        along = dot(jnp.concatenate([high, low], 0), wu_refs[s][...], ((1,), (0,)))
        along = along[: 2 * rows_v] + along[2 * rows_v :]
        wv = weights(meta_refs[s][1:2, :], rows_v)
        real = jnp.sum(along[:rows_v] * wv, 0, keepdims=True)
        imag = jnp.sum(along[rows_v:] * wv, 0, keepdims=True)
        place = (at_ref[0] - s) & (groups - 1)
        part_ref[place] = jnp.concatenate([real, imag], 0)


def backward_kernel(at_ref, part_ref, e_ref, tc_ref, ts_ref, d_ref, *refs):
    groups = (len(refs) - 5) // 2
    meta_refs, wu_refs = refs[:groups], refs[groups : 2 * groups]
    res_ref, out_ref, pred_ref, rs_ref, im_ref = refs[2 * groups :]
    slots = res_ref.shape[1]
    half = d_ref.shape[0] // 2
    band = 2 * groups
    rows_v = rs_ref.shape[1] // band
    pred_ref[...] = jnp.sum(part_ref[...], 0)
    slot = lax.broadcasted_iota(jnp.int32, (2, slots), 1).astype(F32)
    for s in range(groups):
        place = (at_ref[0] - s) & (groups - 1)
        meta = meta_refs[s]
        seen = meta[2:4, :] - pred_ref[place]
        residual = jnp.where(slot < meta[5:6, :], seen, F32(0.0))
        if s == 0:
            res_ref[...] = residual
        wv = weights(meta[1:2, :], rows_v)
        spread = jnp.concatenate([wv * residual[0:1], wv * residual[1:2]], 0).astype(BF)
        cells = dot(spread, wu_refs[s][...], ((1,), (1,)))
        for k in range(KB):
            rs_ref[k, s * 2 * rows_v : (s + 1) * 2 * rows_v, :] = cells[:, k * RES : (k + 1) * RES]
    for v in range(rows_v):
        rows = [rs_ref[k, pl.ds(v, band, stride=rows_v), :] for k in range(KB)]
        cells = jnp.concatenate(rows, 0).astype(BF)
        back = dot(jnp.concatenate([cells, cells], 0), e_ref[...], ((0,), (0,)))
        real_b, imag_b = back[:, :SG], back[:, SG:]
        cos, sin = tc_ref[...], ts_ref[...]
        real_m = (real_b * cos - imag_b * sin).astype(BF)
        imag_m = (imag_b * cos + real_b * sin).astype(BF)
        image = dot(d_ref[...], jnp.concatenate([real_m, imag_m], 0), ((1,), (0,)))
        image = image[:half] + image[half:]
        for k in range(KB):
            im_ref[k, pl.ds(v, half, stride=rows_v), :] = image[:, k * RES : (k + 1) * RES]
    for k in range(KB):
        out_ref[:, k * RES : (k + 1) * RES] = im_ref[k].astype(BF)


def shards(facet_data, subgrid_pos, vis_counts, vis_u_fine, vis_v_fine, vis_observed):
    facets = lax.axis_size("facet")
    subs = lax.axis_size("sub")
    rows_v = facet_data.shape[1]
    slots = vis_u_fine.shape[1]
    facet = lax.axis_index("facet")
    inside = jnp.arange(SG, dtype=jnp.int32)
    residue = jnp.arange(RES, dtype=jnp.int32)

    gathered = gather_by_exchange(facet_data, "sub")

    def wide(value):
        return jnp.broadcast_to(value.astype(F32)[:, None], (1, slots))

    meta = jnp.concatenate(
        [
            vis_u_fine.astype(F32),
            vis_v_fine.astype(F32),
            vis_observed[0],
            vis_observed[1],
            wide(subgrid_pos // RES),
            wide(vis_counts),
            jnp.zeros((ROWS - 6, slots), F32),
        ],
        0,
    )
    metas = [meta]
    for d in range(1, facets):
        ring = [(n, (n + d) % facets) for n in range(facets)]
        metas.append(lax.ppermute(meta, "facet", ring))
    weight_u = [weights(m[0:1], SG).astype(BF) for m in metas]

    table = block_tables(facets, subs)
    high_d, low_d = host_split(table)
    into = jnp.asarray(np.concatenate([high_d, low_d], 2))
    outof = jnp.asarray(np.concatenate([high_d, low_d], 2).transpose(0, 2, 1))
    into = lax.dynamic_index_in_dim(into, facet, 0, keepdims=False)
    outof = lax.dynamic_index_in_dim(outof, facet, 0, keepdims=False)
    turn = (residue[:, None] * inside[None, :]).astype(F32) * (2.0 * math.pi / 65536)
    tw_cos, tw_sin = jnp.cos(turn), jnp.sin(turn)
    spot = jnp.concatenate([m[4:5] for m in metas], 0).astype(jnp.int32)
    step = spot[None] + jnp.arange(KB, dtype=jnp.int32)[:, None, None]
    turn = (step * inside).reshape(KB * facets, SG) % SG
    angle = turn.astype(F32) * (2.0 * math.pi / SG)
    scale = F32(1.0 / 256.0)
    cos, sin = jnp.cos(angle) * scale, jnp.sin(angle) * scale
    lines = jnp.stack(
        [jnp.concatenate([cos, sin], 1), jnp.concatenate([-sin, cos], 1)], 1
    ).reshape(2 * KB * facets, 2 * SG)
    high_e, low_e = split(lines)
    e_table = jnp.concatenate([high_e, low_e], 0)

    at = facet.astype(jnp.int32)[None]
    vmem = pl.BlockSpec(memory_space=pltpu.VMEM)
    smem = pl.BlockSpec(memory_space=pltpu.SMEM)
    part = pl.pallas_call(
        forward_kernel,
        out_shape=jax.ShapeDtypeStruct((facets, 2, slots), F32),
        in_specs=[smem] + [vmem] * (5 + 2 * facets),
        scratch_shapes=[
            pltpu.VMEM((KB, 2 * subs * rows_v, RES), F32),
            pltpu.VMEM((KB, 2 * facets * rows_v, RES), F32),
        ],
        name="forward_share",
    )(
        at, gathered.reshape(2 * subs * rows_v, SG), into, tw_cos, tw_sin, e_table,
        *metas, *weight_u,
    )

    parts = gather_by_exchange(part, "facet")

    residual, image = pl.pallas_call(
        backward_kernel,
        out_shape=(
            jax.ShapeDtypeStruct((2, slots), F32),
            jax.ShapeDtypeStruct((2 * subs * rows_v, SG), BF),
        ),
        in_specs=[smem] + [vmem] * (5 + 2 * facets),
        scratch_shapes=[
            pltpu.VMEM((facets, 2, slots), F32),
            pltpu.VMEM((KB, 2 * facets * rows_v, RES), F32),
            pltpu.VMEM((KB, 2 * subs * rows_v, RES), F32),
        ],
        name="backward_share",
    )(at, parts, e_table, tw_cos, tw_sin, outof, *metas, *weight_u)

    image = image.reshape(subs, 2, rows_v, SG)
    image = lax.all_to_all(image, "sub", 0, 0, tiled=True)
    return (residual[:, None], jnp.sum(image.astype(F32), 0))


def solution(mesh):
    return jax.shard_map(
        shards,
        mesh=mesh,
        in_specs=(
            P(None, None, ("facet", "sub")),
            P(("facet", "sub")),
            P(("facet", "sub")),
            P(("facet", "sub"), None),
            P(("facet", "sub"), None),
            P(None, ("facet", "sub"), None),
        ),
        out_specs=(P(None, ("facet", "sub"), None), P(None, None, ("facet", "sub"))),
        check_vma=False,
    )
```

```python
import math

import jax
import jax.numpy as jnp
import numpy as np
from jax import lax
from jax.experimental import pallas as pl
from jax.experimental.pallas import tpu as pltpu
from jax.sharding import PartitionSpec as P

SG = 512
KS = 8
OVER = 16
RES = 128
KB = SG // RES
ROWS = 8
BF = jnp.bfloat16
F32 = jnp.float32


def split(value):
    high = lax.reduce_precision(value, 8, 7)
    return high.astype(BF), (value - high).astype(BF)


def gather_by_exchange(value, axis):
    count = lax.axis_size(axis)
    copies = jnp.broadcast_to(value[None], (count,) + value.shape)
    return lax.all_to_all(copies, axis, 0, 0, tiled=True)


def block_tables(facets, subs):
    block = np.arange(facets * subs).reshape(facets, subs)
    turn = (np.arange(RES)[None, :, None] * block[:, None, :]) % RES
    angle = turn * (2.0 * math.pi / RES)
    cos, sin = np.cos(angle), np.sin(angle)
    top = np.stack([cos, sin], -1)
    low = np.stack([-sin, cos], -1)
    table = np.concatenate([top, low], 1).reshape(facets, 2 * RES, 2 * subs)
    return table.astype(np.float32)


def host_split(table):
    high = table.astype(jnp.bfloat16)
    return high, (table - high.astype(np.float32)).astype(jnp.bfloat16)


def weights(fine_index, cells):
    middle = fine_index / OVER + (KS - 1) / 2.0
    cell = jnp.floor(fine_index / OVER)
    row = lax.broadcasted_iota(jnp.int32, (cells, fine_index.shape[1]), 0).astype(F32)
    distance = (row - middle) / 0.6
    weight = jnp.exp(-0.5 * (distance * distance))
    return jnp.where((row >= cell) & (row < cell + KS), weight, F32(0.0))


def weight_rows(fine_index, cells):
    cell = jnp.floor(fine_index / OVER)
    tile = jnp.floor(cell / KS)
    inner = cell - tile * KS
    row = lax.broadcasted_iota(jnp.int32, (KS, fine_index.shape[1]), 0).astype(F32)
    wrapped = row < inner
    offset = row - inner + jnp.where(wrapped, F32(KS), F32(0.0))
    distance = (offset - ((KS - 1) / 2.0 + (fine_index / OVER - cell))) / 0.6
    weight = jnp.exp(-0.5 * (distance * distance))
    tile = tile + jnp.where(wrapped, F32(1.0), F32(0.0))
    return [jnp.where(tile == F32(n), weight, F32(0.0)) for n in range(cells // KS)]


def dot(left, right, dims):
    return lax.dot_general(left, right, (dims, ((), ())), preferred_element_type=F32)


def expand(wu_ref, fine_index):
    rows = weight_rows(fine_index, wu_ref.shape[0])
    for n in range(0, len(rows), 2):
        wu_ref[n * KS : (n + 2) * KS, :] = jnp.concatenate(rows[n : n + 2], 0).astype(BF)


def forward_kernel(at_ref, y_ref, d_ref, tc_ref, ts_ref, e_ref, *refs):
    meta_refs = refs[:-4]
    part_ref, ys_ref, gs_ref, wu_ref = refs[-4:]
    groups = len(meta_refs)
    d_table = d_ref[at_ref[0]]
    pieces = y_ref.shape[0]
    half = e_ref.shape[0] // 2
    band = half // KB
    rows_v = gs_ref.shape[1] // band
    lines = pieces // rows_v
    for k in range(KB):
        ys_ref[k] = y_ref[:, k * RES : (k + 1) * RES].astype(F32)
    for v in range(rows_v):
        row = [ys_ref[k, pl.ds(v, lines, stride=rows_v), :] for k in range(KB)]
        row = jnp.concatenate(row, 1).astype(BF)
        spread = dot(d_table, jnp.concatenate([row, row], 0), ((1,), (0,)))
        real_g, imag_g = spread[:RES], spread[RES:]
        cos, sin = tc_ref[...], ts_ref[...]
        real_h = (real_g * cos + imag_g * sin).astype(BF)
        imag_h = (imag_g * cos - real_g * sin).astype(BF)
        share = dot(e_ref[...], jnp.concatenate([real_h, imag_h], 1), ((1,), (1,)))
        share = share[:half] + share[half:]
        for k in range(KB):
            gs_ref[k, pl.ds(v, band, stride=rows_v), :] = share[k * band : (k + 1) * band]
    for s in range(groups):
        grid = [gs_ref[k, s * 2 * rows_v : (s + 1) * 2 * rows_v, :] for k in range(KB)]
        grid = jnp.concatenate(grid, 1)
        high = grid.astype(BF)
        low = (grid - high.astype(F32)).astype(BF)
        expand(wu_ref.at[s], meta_refs[s][0:1, :])
        along = dot(jnp.concatenate([high, low], 0), wu_ref[s], ((1,), (0,)))
        along = along[: 2 * rows_v] + along[2 * rows_v :]
        wv = weights(meta_refs[s][1:2, :], rows_v)
        real = jnp.sum(along[:rows_v] * wv, 0, keepdims=True)
        imag = jnp.sum(along[rows_v:] * wv, 0, keepdims=True)
        place = (at_ref[0] - s) & (groups - 1)
        both = jnp.concatenate([real, imag], 0)
        for n in range(groups):
            part_ref[n, place] = both


def backward_kernel(at_ref, part_ref, e_ref, tc_ref, ts_ref, d_ref, *refs):
    meta_refs = refs[:-6]
    res_ref, out_ref, pred_ref, rs_ref, im_ref, wu_ref = refs[-6:]
    groups = len(meta_refs)
    slots = res_ref.shape[1]
    d_table = d_ref[at_ref[0]]
    half = d_table.shape[0] // 2
    band = 2 * groups
    rows_v = rs_ref.shape[1] // band
    pred_ref[...] = jnp.sum(part_ref[...], 0)
    slot = lax.broadcasted_iota(jnp.int32, (2, slots), 1).astype(F32)
    for s in range(groups):
        place = (at_ref[0] - s) & (groups - 1)
        meta = meta_refs[s]
        seen = meta[2:4, :] - pred_ref[place]
        residual = jnp.where(slot < meta[5:6, :], seen, F32(0.0))
        if s == 0:
            res_ref[...] = residual
        wv = weights(meta[1:2, :], rows_v)
        spread = jnp.concatenate([wv * residual[0:1], wv * residual[1:2]], 0).astype(BF)
        expand(wu_ref.at[s], meta[0:1, :])
        cells = dot(spread, wu_ref[s], ((1,), (1,)))
        for k in range(KB):
            rs_ref[k, s * 2 * rows_v : (s + 1) * 2 * rows_v, :] = cells[:, k * RES : (k + 1) * RES]
    for v in range(rows_v):
        rows = [rs_ref[k, pl.ds(v, band, stride=rows_v), :] for k in range(KB)]
        cells = jnp.concatenate(rows, 0).astype(BF)
        back = dot(jnp.concatenate([cells, cells], 0), e_ref[...], ((0,), (0,)))
        real_b, imag_b = back[:, :SG], back[:, SG:]
        cos, sin = tc_ref[...], ts_ref[...]
        real_m = (real_b * cos - imag_b * sin).astype(BF)
        imag_m = (imag_b * cos + real_b * sin).astype(BF)
        image = dot(d_table, jnp.concatenate([real_m, imag_m], 0), ((1,), (0,)))
        image = image[:half] + image[half:]
        for k in range(KB):
            im_ref[k, pl.ds(v, half, stride=rows_v), :] = image[:, k * RES : (k + 1) * RES]
    for k in range(KB):
        out_ref[:, k * RES : (k + 1) * RES] = im_ref[k].astype(BF)


def shards(facet_data, subgrid_pos, vis_counts, vis_u_fine, vis_v_fine, vis_observed):
    facets = lax.axis_size("facet")
    subs = lax.axis_size("sub")
    rows_v = facet_data.shape[1]
    slots = vis_u_fine.shape[1]
    facet = lax.axis_index("facet")
    inside = jnp.arange(SG, dtype=jnp.int32)

    gathered = gather_by_exchange(facet_data, "sub")

    def wide(value):
        return jnp.broadcast_to(value.astype(F32)[:, None], (1, slots))

    meta = jnp.concatenate(
        [
            vis_u_fine.astype(F32),
            vis_v_fine.astype(F32),
            vis_observed[0],
            vis_observed[1],
            wide(subgrid_pos // RES),
            wide(vis_counts),
            jnp.zeros((ROWS - 6, slots), F32),
        ],
        0,
    )
    metas = [meta]
    for d in range(1, facets):
        ring = [(n, (n + d) % facets) for n in range(facets)]
        metas.append(lax.ppermute(meta, "facet", ring))

    table = block_tables(facets, subs)
    high_d, low_d = host_split(table)
    into = jnp.asarray(np.concatenate([high_d, low_d], 2))
    outof = jnp.asarray(np.concatenate([high_d, low_d], 2).transpose(0, 2, 1))
    turn = np.arange(RES)[:, None] * np.arange(SG)[None, :] * (2.0 * math.pi / 65536)
    tw_cos = jnp.asarray(np.cos(turn).astype(np.float32))
    tw_sin = jnp.asarray(np.sin(turn).astype(np.float32))
    spot = jnp.concatenate([m[4:5] for m in metas], 0).astype(jnp.int32)
    step = spot[None] + jnp.arange(KB, dtype=jnp.int32)[:, None, None]
    turn = (step * inside).reshape(KB * facets, SG) % SG
    angle = turn.astype(F32) * (2.0 * math.pi / SG)
    scale = F32(1.0 / 256.0)
    cos, sin = jnp.cos(angle) * scale, jnp.sin(angle) * scale
    lines = jnp.stack(
        [jnp.concatenate([cos, sin], 1), jnp.concatenate([-sin, cos], 1)], 1
    ).reshape(2 * KB * facets, 2 * SG)
    high_e, low_e = split(lines)
    e_table = jnp.concatenate([high_e, low_e], 0)

    at = facet.astype(jnp.int32)[None]
    params = pltpu.CompilerParams(vmem_limit_bytes=24 * 1024 * 1024)
    vmem = pl.BlockSpec(memory_space=pltpu.VMEM)
    smem = pl.BlockSpec(memory_space=pltpu.SMEM)
    part = pl.pallas_call(
        forward_kernel,
        out_shape=jax.ShapeDtypeStruct((facets, facets, 2, slots), F32),
        in_specs=[smem] + [vmem] * (5 + facets),
        scratch_shapes=[
            pltpu.VMEM((KB, 2 * subs * rows_v, RES), F32),
            pltpu.VMEM((KB, 2 * facets * rows_v, RES), F32),
            pltpu.VMEM((facets, SG, slots), BF),
        ],
        compiler_params=params,
        name="forward_share",
    )(
        at, gathered.reshape(2 * subs * rows_v, SG), into, tw_cos, tw_sin, e_table,
        *metas,
    )

    parts = lax.all_to_all(part, "facet", 0, 0, tiled=True)

    residual, image = pl.pallas_call(
        backward_kernel,
        out_shape=(
            jax.ShapeDtypeStruct((2, slots), F32),
            jax.ShapeDtypeStruct((2 * subs * rows_v, SG), BF),
        ),
        in_specs=[smem] + [vmem] * (5 + facets),
        scratch_shapes=[
            pltpu.VMEM((facets, 2, slots), F32),
            pltpu.VMEM((KB, 2 * facets * rows_v, RES), F32),
            pltpu.VMEM((KB, 2 * subs * rows_v, RES), F32),
            pltpu.VMEM((facets, SG, slots), BF),
        ],
        compiler_params=params,
        name="backward_share",
    )(at, parts, e_table, tw_cos, tw_sin, outof, *metas)

    image = image.reshape(subs, 2, rows_v, SG)
    image = lax.all_to_all(image, "sub", 0, 0, tiled=True)
    return (residual[:, None], jnp.sum(image.astype(F32), 0))


def solution(mesh):
    return jax.shard_map(
        shards,
        mesh=mesh,
        in_specs=(
            P(None, None, ("facet", "sub")),
            P(("facet", "sub")),
            P(("facet", "sub")),
            P(("facet", "sub"), None),
            P(("facet", "sub"), None),
            P(None, ("facet", "sub"), None),
        ),
        out_specs=(P(None, ("facet", "sub"), None), P(None, None, ("facet", "sub"))),
        check_vma=False,
    )
```

```python
import math

import jax
import jax.numpy as jnp
import numpy as np
from jax import lax
from jax.experimental import pallas as pl
from jax.experimental.pallas import tpu as pltpu
from jax.sharding import PartitionSpec as P

SG = 512
KS = 8
OVER = 16
RES = 128
KB = SG // RES
BATCH = 2
ROWS = 8
BF = jnp.bfloat16
F32 = jnp.float32


def split(value):
    high = lax.reduce_precision(value, 8, 7)
    return high.astype(BF), (value - high).astype(BF)


def gather_by_exchange(value, axis):
    count = lax.axis_size(axis)
    copies = jnp.broadcast_to(value[None], (count,) + value.shape)
    return lax.all_to_all(copies, axis, 0, 0, tiled=True)


def block_tables(facets, subs):
    block = np.arange(facets * subs).reshape(facets, subs)
    turn = (np.arange(RES)[None, :, None] * block[:, None, :]) % RES
    angle = turn * (2.0 * math.pi / RES)
    cos, sin = np.cos(angle), np.sin(angle)
    top = np.stack([cos, sin], -1)
    low = np.stack([-sin, cos], -1)
    table = np.concatenate([top, low], 1).reshape(facets, 2 * RES, 2 * subs)
    return table.astype(np.float32)


def host_split(table):
    high = table.astype(jnp.bfloat16)
    return high, (table - high.astype(np.float32)).astype(jnp.bfloat16)


def weights(fine_index, cells):
    middle = fine_index / OVER + (KS - 1) / 2.0
    cell = jnp.floor(fine_index / OVER)
    row = lax.broadcasted_iota(jnp.int32, (cells, fine_index.shape[1]), 0).astype(F32)
    distance = (row - middle) / 0.6
    weight = jnp.exp(-0.5 * (distance * distance))
    return jnp.where((row >= cell) & (row < cell + KS), weight, F32(0.0))


def weight_rows(fine_index, cells):
    cell = jnp.floor(fine_index / OVER)
    tile = jnp.floor(cell / KS)
    inner = cell - tile * KS
    row = lax.broadcasted_iota(jnp.int32, (KS, fine_index.shape[1]), 0).astype(F32)
    wrapped = row < inner
    offset = row - inner + jnp.where(wrapped, F32(KS), F32(0.0))
    distance = (offset - ((KS - 1) / 2.0 + (fine_index / OVER - cell))) / 0.6
    weight = jnp.exp(-0.5 * (distance * distance))
    tile = tile + jnp.where(wrapped, F32(1.0), F32(0.0))
    return [jnp.where(tile == F32(n), weight, F32(0.0)) for n in range(cells // KS)]


def dot(left, right, dims):
    return lax.dot_general(left, right, (dims, ((), ())), preferred_element_type=F32)


def expand(wu_ref, fine_index):
    rows = weight_rows(fine_index, wu_ref.shape[0])
    for n in range(0, len(rows), 2):
        wu_ref[n * KS : (n + 2) * KS, :] = jnp.concatenate(rows[n : n + 2], 0).astype(BF)


def forward_kernel(at_ref, y_ref, d_ref, tc_ref, ts_ref, e_ref, *refs):
    meta_refs = refs[:-4]
    part_ref, ys_ref, gs_ref, wu_ref = refs[-4:]
    groups = len(meta_refs)
    d_table = d_ref[at_ref[0]]
    pieces = y_ref.shape[0]
    half = e_ref.shape[0] // 2
    band = half // KB
    rows_v = gs_ref.shape[1] // band
    lines = pieces // rows_v
    for k in range(KB):
        ys_ref[k] = y_ref[:, k * RES : (k + 1) * RES].astype(F32)
    for v in range(rows_v):
        row = [ys_ref[k, pl.ds(v, lines, stride=rows_v), :] for k in range(KB)]
        row = jnp.concatenate(row, 1).astype(BF)
        spread = dot(d_table, jnp.concatenate([row, row], 0), ((1,), (0,)))
        real_g, imag_g = spread[:RES], spread[RES:]
        cos, sin = tc_ref[...], ts_ref[...]
        real_h = (real_g * cos + imag_g * sin).astype(BF)
        imag_h = (imag_g * cos - real_g * sin).astype(BF)
        share = dot(e_ref[...], jnp.concatenate([real_h, imag_h], 1), ((1,), (1,)))
        share = share[:half] + share[half:]
        for k in range(KB):
            gs_ref[k, pl.ds(v, band, stride=rows_v), :] = share[k * band : (k + 1) * band]
    for s in range(groups):
        grid = [gs_ref[k, s * 2 * rows_v : (s + 1) * 2 * rows_v, :] for k in range(KB)]
        grid = jnp.concatenate(grid, 1)
        high = grid.astype(BF)
        low = (grid - high.astype(F32)).astype(BF)
        expand(wu_ref.at[s], meta_refs[s][0:1, :])
        along = dot(jnp.concatenate([high, low], 0), wu_ref[s], ((1,), (0,)))
        along = along[: 2 * rows_v] + along[2 * rows_v :]
        wv = weights(meta_refs[s][1:2, :], rows_v)
        real = jnp.sum(along[:rows_v] * wv, 0, keepdims=True)
        imag = jnp.sum(along[rows_v:] * wv, 0, keepdims=True)
        place = (at_ref[0] - s) & (groups - 1)
        both = jnp.concatenate([real, imag], 0).astype(BF)
        for n in range(groups):
            part_ref[n, place] = both


def backward_kernel(at_ref, part_ref, e_ref, tc_ref, ts_ref, d_ref, *refs):
    meta_refs = refs[:-6]
    res_ref, out_ref, pred_ref, rs_ref, im_ref, wu_ref = refs[-6:]
    groups = len(meta_refs)
    slots = res_ref.shape[1]
    d_table = d_ref[at_ref[0]]
    lines = d_table.shape[0]
    band = 2 * groups
    rows_v = rs_ref.shape[1] // band
    pred_ref[...] = jnp.sum(part_ref[...].astype(F32), 0)
    slot = lax.broadcasted_iota(jnp.int32, (2, slots), 1).astype(F32)
    for s in range(groups):
        place = (at_ref[0] - s) & (groups - 1)
        meta = meta_refs[s]
        seen = meta[2:4, :] - pred_ref[place]
        residual = jnp.where(slot < meta[5:6, :], seen, F32(0.0))
        if s == 0:
            res_ref[...] = residual
        wv = weights(meta[1:2, :], rows_v)
        spread = jnp.concatenate([wv * residual[0:1], wv * residual[1:2]], 0).astype(BF)
        expand(wu_ref.at[s], meta[0:1, :])
        cells = dot(spread, wu_ref[s], ((1,), (1,)))
        for k in range(KB):
            rs_ref[k, s * 2 * rows_v : (s + 1) * 2 * rows_v, :] = cells[:, k * RES : (k + 1) * RES]
    e_table = e_ref[: KB * band, :]
    for v in range(0, rows_v, BATCH):
        cells = []
        for n in range(BATCH):
            rows = [rs_ref[k, pl.ds(v + n, band, stride=rows_v), :] for k in range(KB)]
            cells.append(jnp.concatenate(rows, 0))
        cells = jnp.concatenate(cells, 1).astype(BF)
        back = dot(cells, e_table, ((0,), (0,)))
        for n in range(BATCH):
            real_b, imag_b = jnp.split(back[n * RES : (n + 1) * RES], 2, 1)
            cos, sin = tc_ref[...], ts_ref[...]
            real_m = (real_b * cos - imag_b * sin).astype(BF)
            imag_m = (imag_b * cos + real_b * sin).astype(BF)
            image = dot(d_table, jnp.concatenate([real_m, imag_m], 0), ((1,), (0,)))
            for k in range(KB):
                im_ref[k, pl.ds(v + n, lines, stride=rows_v), :] = image[
                    :, k * RES : (k + 1) * RES
                ]
    for k in range(KB):
        out_ref[:, k * RES : (k + 1) * RES] = im_ref[k].astype(BF)


def shards(facet_data, subgrid_pos, vis_counts, vis_u_fine, vis_v_fine, vis_observed):
    facets = lax.axis_size("facet")
    subs = lax.axis_size("sub")
    rows_v = facet_data.shape[1]
    slots = vis_u_fine.shape[1]
    facet = lax.axis_index("facet")
    inside = jnp.arange(SG, dtype=jnp.int32)

    gathered = gather_by_exchange(facet_data, "sub")

    def wide(value):
        return jnp.broadcast_to(value.astype(F32)[:, None], (1, slots))

    meta = jnp.concatenate(
        [
            vis_u_fine.astype(F32),
            vis_v_fine.astype(F32),
            vis_observed[0],
            vis_observed[1],
            wide(subgrid_pos // RES),
            wide(vis_counts),
            jnp.zeros((ROWS - 6, slots), F32),
        ],
        0,
    )
    metas = [meta]
    for d in range(1, facets):
        ring = [(n, (n + d) % facets) for n in range(facets)]
        metas.append(lax.ppermute(meta, "facet", ring))

    table = block_tables(facets, subs)
    high_d, low_d = host_split(table)
    into = jnp.asarray(np.concatenate([high_d, low_d], 2))
    outof = jnp.asarray(high_d.transpose(0, 2, 1))
    turn = np.arange(RES)[:, None] * np.arange(SG)[None, :] * (2.0 * math.pi / 65536)
    tw_cos = jnp.asarray(np.cos(turn).astype(np.float32))
    tw_sin = jnp.asarray(np.sin(turn).astype(np.float32))
    spot = jnp.concatenate([m[4:5] for m in metas], 0).astype(jnp.int32)
    step = spot[None] + jnp.arange(KB, dtype=jnp.int32)[:, None, None]
    turn = (step * inside).reshape(KB * facets, SG) % SG
    angle = turn.astype(F32) * (2.0 * math.pi / SG)
    scale = F32(1.0 / 256.0)
    cos, sin = jnp.cos(angle) * scale, jnp.sin(angle) * scale
    lines = jnp.stack(
        [jnp.concatenate([cos, sin], 1), jnp.concatenate([-sin, cos], 1)], 1
    ).reshape(2 * KB * facets, 2 * SG)
    high_e, low_e = split(lines)
    e_table = jnp.concatenate([high_e, low_e], 0)

    at = facet.astype(jnp.int32)[None]
    params = pltpu.CompilerParams(vmem_limit_bytes=24 * 1024 * 1024)
    vmem = pl.BlockSpec(memory_space=pltpu.VMEM)
    smem = pl.BlockSpec(memory_space=pltpu.SMEM)
    part = pl.pallas_call(
        forward_kernel,
        out_shape=jax.ShapeDtypeStruct((facets, facets, 2, slots), BF),
        in_specs=[smem] + [vmem] * (5 + facets),
        scratch_shapes=[
            pltpu.VMEM((KB, 2 * subs * rows_v, RES), F32),
            pltpu.VMEM((KB, 2 * facets * rows_v, RES), F32),
            pltpu.VMEM((facets, SG, slots), BF),
        ],
        compiler_params=params,
        name="forward_share",
    )(
        at, gathered.reshape(2 * subs * rows_v, SG), into, tw_cos, tw_sin, e_table,
        *metas,
    )

    parts = lax.all_to_all(part, "facet", 0, 0, tiled=True)

    residual, image = pl.pallas_call(
        backward_kernel,
        out_shape=(
            jax.ShapeDtypeStruct((2, slots), F32),
            jax.ShapeDtypeStruct((2 * subs * rows_v, SG), BF),
        ),
        in_specs=[smem] + [vmem] * (5 + facets),
        scratch_shapes=[
            pltpu.VMEM((facets, 2, slots), F32),
            pltpu.VMEM((KB, 2 * facets * rows_v, RES), F32),
            pltpu.VMEM((KB, 2 * subs * rows_v, RES), F32),
            pltpu.VMEM((facets, SG, slots), BF),
        ],
        compiler_params=params,
        name="backward_share",
    )(at, parts, e_table, tw_cos, tw_sin, outof, *metas)

    image = image.reshape(subs, 2, rows_v, SG)
    image = lax.all_to_all(image, "sub", 0, 0, tiled=True)
    return (residual[:, None], jnp.sum(image.astype(F32), 0))


def solution(mesh):
    return jax.shard_map(
        shards,
        mesh=mesh,
        in_specs=(
            P(None, None, ("facet", "sub")),
            P(("facet", "sub")),
            P(("facet", "sub")),
            P(("facet", "sub"), None),
            P(("facet", "sub"), None),
            P(None, ("facet", "sub"), None),
        ),
        out_specs=(P(None, ("facet", "sub"), None), P(None, None, ("facet", "sub"))),
        check_vma=False,
    )
```

```python
import math

import jax
import jax.numpy as jnp
import numpy as np
from jax import lax
from jax.experimental import pallas as pl
from jax.experimental.pallas import tpu as pltpu
from jax.sharding import PartitionSpec as P

SG = 512
KS = 8
OVER = 16
RES = 128
KB = SG // RES
BATCH = 2
CHUNK = 16
WAVE = 8
SUB = 8
ROWS = 8
BF = jnp.bfloat16
F32 = jnp.float32


def split(value):
    high = lax.reduce_precision(value, 8, 7)
    return high.astype(BF), (value - high).astype(BF)


def gather_by_exchange(value, axis):
    count = lax.axis_size(axis)
    copies = jnp.broadcast_to(value[None], (count,) + value.shape)
    return lax.all_to_all(copies, axis, 0, 0, tiled=True)


def block_tables(facets, subs):
    block = np.arange(facets * subs).reshape(facets, subs)
    turn = (np.arange(RES)[None, :, None] * block[:, None, :]) % RES
    angle = turn * (2.0 * math.pi / RES)
    cos, sin = np.cos(angle), np.sin(angle)
    top = np.stack([cos, sin], -1)
    low = np.stack([-sin, cos], -1)
    table = np.concatenate([top, low], 1).reshape(facets, 2 * RES, 2 * subs)
    return table.astype(np.float32)


def host_split(table):
    high = table.astype(jnp.bfloat16)
    return high, (table - high.astype(np.float32)).astype(jnp.bfloat16)


def weights(fine_index, cells):
    middle = fine_index / OVER + (KS - 1) / 2.0
    cell = jnp.floor(fine_index / OVER)
    row = lax.broadcasted_iota(jnp.int32, (cells, fine_index.shape[1]), 0).astype(F32)
    distance = (row - middle) / 0.6
    weight = jnp.exp(-0.5 * (distance * distance))
    return jnp.where((row >= cell) & (row < cell + KS), weight, F32(0.0))


def weight_rows(fine_index, cells):
    cell = jnp.floor(fine_index / OVER)
    tile = jnp.floor(cell / KS)
    inner = cell - tile * KS
    row = lax.broadcasted_iota(jnp.int32, (KS, fine_index.shape[1]), 0).astype(F32)
    wrapped = row < inner
    offset = row - inner + jnp.where(wrapped, F32(KS), F32(0.0))
    distance = (offset - ((KS - 1) / 2.0 + (fine_index / OVER - cell))) / 0.6
    weight = jnp.exp(-0.5 * (distance * distance))
    tile = tile + jnp.where(wrapped, F32(1.0), F32(0.0))
    return [jnp.where(tile == F32(n), weight, F32(0.0)) for n in range(cells // KS)]


def dot(left, right, dims):
    return lax.dot_general(left, right, (dims, ((), ())), preferred_element_type=F32)


def slot_rows(refs, slot):
    start = (slot % 2) * ROWS
    return refs[slot // 2], start


def slot_place(at, slot, groups):
    return ((at - (slot // 2) * 2) & (groups - 1)) ^ (slot % 2)


def pack_kernel(pos_ref, cnt_ref, u_ref, v_ref, obs_ref, *refs):
    meta_ref = refs[-1]
    slots = u_ref.shape[1]
    meta_ref[0:1, :] = u_ref[...].astype(F32)
    meta_ref[1:2, :] = v_ref[...].astype(F32)
    meta_ref[2:3, :] = obs_ref[0]
    meta_ref[3:4, :] = obs_ref[1]
    meta_ref[4:5, :] = jnp.full((1, slots), pos_ref[0] // RES, jnp.int32).astype(F32)
    meta_ref[5:6, :] = jnp.full((1, slots), cnt_ref[0], jnp.int32).astype(F32)
    meta_ref[6:8, :] = jnp.zeros((2, slots), F32)


def expand(wu_ref, fine_index):
    rows = weight_rows(fine_index, wu_ref.shape[0])
    for n in range(0, len(rows), 2):
        wu_ref[n * KS : (n + 2) * KS, :] = jnp.concatenate(rows[n : n + 2], 0).astype(BF)


def forward_kernel(at_ref, y_ref, d_ref, tc_ref, ts_ref, e_ref, *refs):
    meta_refs = refs[:-4]
    part_ref, ys_ref, gs_ref, wu_ref = refs[-4:]
    groups = 2 * len(meta_refs)
    d_table = d_ref[at_ref[0]]
    pieces = y_ref.shape[0]
    half = e_ref.shape[0] // 2
    band = half // KB
    rows_v = gs_ref.shape[1] // band
    lines = pieces // rows_v
    for k in range(KB):
        ys_ref[k] = y_ref[:, k * RES : (k + 1) * RES].astype(F32)
    for v in range(0, rows_v, BATCH):
        turned = []
        for n in range(BATCH):
            row = [ys_ref[k, pl.ds(v + n, lines, stride=rows_v), :] for k in range(KB)]
            row = jnp.concatenate(row, 1).astype(BF)
            spread = dot(d_table, jnp.concatenate([row, row], 0), ((1,), (0,)))
            spread = spread.reshape(RES // SUB, 2, SUB, SG)
            real_g, imag_g = spread[:, 0], spread[:, 1]
            cos = tc_ref[...].reshape(RES // SUB, SUB, SG)
            sin = ts_ref[...].reshape(RES // SUB, SUB, SG)
            real_h = (real_g * cos + imag_g * sin).reshape(RES, SG).astype(BF)
            imag_h = (imag_g * cos - real_g * sin).reshape(RES, SG).astype(BF)
            turned.append(jnp.concatenate([real_h, imag_h], 1))
        share = dot(e_ref[...], jnp.concatenate(turned, 0), ((1,), (1,)))
        share = share[:half] + share[half:]
        for n in range(BATCH):
            for k in range(KB):
                gs_ref[k, pl.ds(v + n, band, stride=rows_v), :] = share[
                    k * band : (k + 1) * band, n * RES : (n + 1) * RES
                ]
    for s in range(groups):
        grid = [gs_ref[k, s * 2 * rows_v : (s + 1) * 2 * rows_v, :] for k in range(KB)]
        grid = jnp.concatenate(grid, 1)
        high = grid.astype(BF)
        low = (grid - high.astype(F32)).astype(BF)
        meta, start = slot_rows(meta_refs, s)
        expand(wu_ref.at[s], meta[start : start + 1, :])
        along = dot(jnp.concatenate([high, low], 0), wu_ref[s], ((1,), (0,)))
        along = along[: 2 * rows_v] + along[2 * rows_v :]
        wv = weights(meta[start + 1 : start + 2, :], rows_v)
        real = jnp.sum(along[:rows_v] * wv, 0, keepdims=True)
        imag = jnp.sum(along[rows_v:] * wv, 0, keepdims=True)
        place = slot_place(at_ref[0], s, groups)
        both = jnp.concatenate([real, imag], 0).astype(BF)
        for n in range(groups):
            part_ref[n, place] = both


def backward_kernel(at_ref, part_ref, e_ref, tc_ref, ts_ref, d_ref, *refs):
    meta_refs = refs[:-8]
    res_ref, out_ref, pred_ref, rs_ref, im_ref, wu_ref, ct_ref, m_ref = refs[-8:]
    groups = 2 * len(meta_refs)
    slots = res_ref.shape[2]
    d_table = d_ref[at_ref[0]]
    lines = d_table.shape[0]
    band = 2 * groups
    rows_v = rs_ref.shape[1] // band
    pred_ref[...] = jnp.sum(part_ref[...].astype(F32), 0)
    slot = lax.broadcasted_iota(jnp.int32, (2, slots), 1).astype(F32)
    for s in range(groups):
        place = slot_place(at_ref[0], s, groups)
        meta, start = slot_rows(meta_refs, s)
        seen = meta[start + 2 : start + 4, :] - pred_ref[place]
        residual = jnp.where(slot < meta[start + 5 : start + 6, :], seen, F32(0.0))
        if s == 0:
            res_ref[0] = residual[0:1]
            res_ref[1] = residual[1:2]
        wv = weights(meta[start + 1 : start + 2, :], rows_v)
        spread = jnp.concatenate([wv * residual[0:1], wv * residual[1:2]], 0).astype(BF)
        expand(wu_ref.at[s], meta[start : start + 1, :])
        cells = dot(spread, wu_ref[s], ((1,), (1,)))
        for k in range(KB):
            rs_ref[k, s * 2 * rows_v : (s + 1) * 2 * rows_v, :] = cells[:, k * RES : (k + 1) * RES]
    for v in range(rows_v):
        rows = [rs_ref[k, pl.ds(v, band, stride=rows_v), :] for k in range(KB)]
        ct_ref[v] = jnp.concatenate(rows, 0).T.astype(BF)
    e_table = e_ref[: KB * band, :]
    for f in range(0, RES, CHUNK):
        cos = tc_ref[f : f + CHUNK, :]
        sin = ts_ref[f : f + CHUNK, :]
        for v in range(0, rows_v, WAVE):
            cells = ct_ref[v : v + WAVE, f : f + CHUNK, :].reshape(WAVE * CHUNK, KB * band)
            back = dot(cells, e_table, ((1,), (0,))).reshape(WAVE, CHUNK, 2 * SG)
            real_b, imag_b = back[..., :SG], back[..., SG:]
            m_ref[v : v + WAVE, f : f + CHUNK, :] = (real_b * cos - imag_b * sin).astype(BF)
            m_ref[v : v + WAVE, RES + f : RES + f + CHUNK, :] = (
                imag_b * cos + real_b * sin
            ).astype(BF)
    for v in range(rows_v):
        image = dot(d_table, m_ref[v], ((1,), (0,)))
        for k in range(KB):
            im_ref[k, pl.ds(v, lines, stride=rows_v), :] = image[:, k * RES : (k + 1) * RES]
    for k in range(KB):
        out_ref[:, k * RES : (k + 1) * RES] = im_ref[k].astype(BF)


def shards(facet_data, subgrid_pos, vis_counts, vis_u_fine, vis_v_fine, vis_observed):
    facets = lax.axis_size("facet")
    subs = lax.axis_size("sub")
    rows_v = facet_data.shape[1]
    slots = vis_u_fine.shape[1]
    facet = lax.axis_index("facet")
    inside = jnp.arange(SG, dtype=jnp.int32)

    gathered = gather_by_exchange(facet_data, "sub")

    table = block_tables(facets, subs)
    high_d, low_d = host_split(table)
    into = np.concatenate([high_d, low_d], 2)
    into = into.reshape(facets, 2, RES // SUB, SUB, -1).swapaxes(1, 2)
    into = jnp.asarray(into.reshape(facets, 2 * RES, -1))
    outof = jnp.asarray(high_d.transpose(0, 2, 1))
    turn = np.arange(RES)[:, None] * np.arange(SG)[None, :] * (2.0 * math.pi / 65536)
    tw_cos = jnp.asarray(np.cos(turn).astype(np.float32))
    tw_sin = jnp.asarray(np.sin(turn).astype(np.float32))
    params = pltpu.CompilerParams(vmem_limit_bytes=24 * 1024 * 1024)
    vmem = pl.BlockSpec(memory_space=pltpu.VMEM)
    smem = pl.BlockSpec(memory_space=pltpu.SMEM)
    meta = pl.pallas_call(
        pack_kernel,
        out_shape=jax.ShapeDtypeStruct((ROWS, slots), F32),
        in_specs=[smem] * 2 + [vmem] * 7,
        out_specs=vmem,
        compiler_params=params,
        name="pack_meta",
    )(
        subgrid_pos, vis_counts, vis_u_fine, vis_v_fine, vis_observed,
        into, outof, tw_cos, tw_sin,
    )
    partner = lax.ppermute(meta, "facet", [(n, n ^ 1) for n in range(facets)])
    pairs = [jnp.concatenate([meta, partner], 0)]
    for d in range(2, facets, 2):
        ring = [(n, (n + d) % facets) for n in range(facets)]
        pairs.append(lax.ppermute(pairs[0], "facet", ring))

    spot = jnp.concatenate([p[n : n + 1] for p in pairs for n in (4, 4 + ROWS)], 0)
    spot = spot.astype(jnp.int32)
    step = spot[None] + jnp.arange(KB, dtype=jnp.int32)[:, None, None]
    turn = (step * inside).reshape(KB * facets, SG) % SG
    angle = turn.astype(F32) * (2.0 * math.pi / SG)
    scale = F32(1.0 / 256.0)
    cos, sin = jnp.cos(angle) * scale, jnp.sin(angle) * scale
    lines = jnp.stack(
        [jnp.concatenate([cos, sin], 1), jnp.concatenate([-sin, cos], 1)], 1
    ).reshape(2 * KB * facets, 2 * SG)
    high_e, low_e = split(lines)
    e_table = jnp.concatenate([high_e, low_e], 0)

    at = facet.astype(jnp.int32)[None]
    part = pl.pallas_call(
        forward_kernel,
        out_shape=jax.ShapeDtypeStruct((facets, facets, 2, slots), BF),
        in_specs=[smem] + [vmem] * (5 + facets // 2),
        scratch_shapes=[
            pltpu.VMEM((KB, 2 * subs * rows_v, RES), F32),
            pltpu.VMEM((KB, 2 * facets * rows_v, RES), F32),
            pltpu.VMEM((facets, SG, slots), BF),
        ],
        compiler_params=params,
        name="forward_share",
    )(
        at, gathered.reshape(2 * subs * rows_v, SG), into, tw_cos, tw_sin, e_table,
        *pairs,
    )

    parts = lax.all_to_all(part, "facet", 0, 0, tiled=True)

    residual, image = pl.pallas_call(
        backward_kernel,
        out_shape=(
            jax.ShapeDtypeStruct((2, 1, slots), F32),
            jax.ShapeDtypeStruct((2 * subs * rows_v, SG), BF),
        ),
        in_specs=[smem] + [vmem] * (5 + facets // 2),
        scratch_shapes=[
            pltpu.VMEM((facets, 2, slots), F32),
            pltpu.VMEM((KB, 2 * facets * rows_v, RES), F32),
            pltpu.VMEM((KB, 2 * subs * rows_v, RES), F32),
            pltpu.VMEM((facets, SG, slots), BF),
            pltpu.VMEM((rows_v, RES, 2 * KB * facets), BF),
            pltpu.VMEM((rows_v, 2 * RES, SG), BF),
        ],
        compiler_params=params,
        name="backward_share",
    )(at, parts, e_table, tw_cos, tw_sin, outof, *pairs)

    image = image.reshape(subs, 2, rows_v, SG)
    image = lax.all_to_all(image, "sub", 0, 0, tiled=True)
    return (residual, jnp.sum(image.astype(F32), 0))


def solution(mesh):
    return jax.shard_map(
        shards,
        mesh=mesh,
        in_specs=(
            P(None, None, ("facet", "sub")),
            P(("facet", "sub")),
            P(("facet", "sub")),
            P(("facet", "sub"), None),
            P(("facet", "sub"), None),
            P(None, ("facet", "sub"), None),
        ),
        out_specs=(P(None, ("facet", "sub"), None), P(None, None, ("facet", "sub"))),
        check_vma=False,
    )
```

```python
import math

import jax
import jax.numpy as jnp
import numpy as np
from jax import lax
from jax.experimental import pallas as pl
from jax.experimental.pallas import tpu as pltpu
from jax.sharding import PartitionSpec as P

SG = 512
KS = 8
OVER = 16
RES = 128
KB = SG // RES
BATCH = 4
CHUNK = 16
WAVE = 4
SUB = 8
ROWS = 8
BF = jnp.bfloat16
F32 = jnp.float32


def block_tables(facets, subs):
    block = np.arange(facets * subs).reshape(facets, subs)
    turn = (np.arange(RES)[None, :, None] * block[:, None, :]) % RES
    angle = turn * (2.0 * math.pi / RES)
    cos, sin = np.cos(angle), np.sin(angle)
    top = np.stack([cos, sin], -1)
    low = np.stack([-sin, cos], -1)
    table = np.concatenate([top, low], 1).reshape(facets, 2 * RES, 2 * subs)
    return table.astype(np.float32)


def host_split(table):
    high = table.astype(jnp.bfloat16)
    return high, (table - high.astype(np.float32)).astype(jnp.bfloat16)


def weights(fine_index, cells):
    middle = fine_index / OVER + (KS - 1) / 2.0
    cell = jnp.floor(fine_index / OVER)
    row = lax.broadcasted_iota(jnp.int32, (cells, fine_index.shape[1]), 0).astype(F32)
    distance = (row - middle) / 0.6
    weight = jnp.exp(-0.5 * (distance * distance))
    return jnp.where((row >= cell) & (row < cell + KS), weight, F32(0.0))


def weight_rows(fine_index, cells):
    cell = jnp.floor(fine_index / OVER)
    tile = jnp.floor(cell / KS)
    inner = cell - tile * KS
    row = lax.broadcasted_iota(jnp.int32, (KS, fine_index.shape[1]), 0).astype(F32)
    wrapped = row < inner
    offset = row - inner + jnp.where(wrapped, F32(KS), F32(0.0))
    distance = (offset - ((KS - 1) / 2.0 + (fine_index / OVER - cell))) / 0.6
    weight = jnp.exp(-0.5 * (distance * distance))
    tile = tile + jnp.where(wrapped, F32(1.0), F32(0.0))
    return [jnp.where(tile == F32(n), weight, F32(0.0)) for n in range(cells // KS)]


def dot(left, right, dims):
    return lax.dot_general(left, right, (dims, ((), ())), preferred_element_type=F32)


def slot_rows(refs, slot):
    start = (slot % 2) * ROWS
    return refs[slot // 2], start


def slot_place(at, slot, groups):
    return ((at - (slot // 2) * 2) & (groups - 1)) ^ (slot % 2)


def lead_kernel(
    pos_ref, cnt_ref, y_hbm, u_hbm, v_hbm, obs_hbm, copy_hbm, meta_ref,
    y_ref, u_ref, v_ref, obs_ref, load_sem, send_sem,
):
    slots = u_ref.shape[1]
    loads = [
        pltpu.make_async_copy(source, target, load_sem.at[n])
        for n, (source, target) in enumerate(
            [(y_hbm, y_ref), (u_hbm, u_ref), (v_hbm, v_ref), (obs_hbm, obs_ref)]
        )
    ]
    for load in loads:
        load.start()
    loads[0].wait()
    sends = [
        pltpu.make_async_copy(y_ref, copy_hbm.at[n], send_sem.at[n])
        for n in range(copy_hbm.shape[0])
    ]
    for send in sends:
        send.start()
    for load in loads[1:]:
        load.wait()
    meta_ref[0:1, :] = u_ref[...].astype(F32)
    meta_ref[1:2, :] = v_ref[...].astype(F32)
    meta_ref[2:3, :] = obs_ref[0]
    meta_ref[3:4, :] = obs_ref[1]
    meta_ref[4:5, :] = jnp.full((1, slots), pos_ref[0] // RES, jnp.int32).astype(F32)
    meta_ref[5:6, :] = jnp.full((1, slots), cnt_ref[0], jnp.int32).astype(F32)
    meta_ref[6:8, :] = jnp.zeros((2, slots), F32)
    for send in sends:
        send.wait()


def table_kernel(*refs):
    e_ref = refs[-1]
    pairs = refs[: len(refs) - 4]
    groups = 2 * len(pairs)
    spot = jnp.concatenate([p[n : n + 1, :] for p in pairs for n in (4, 4 + ROWS)], 0)
    step = jnp.concatenate([spot + F32(k) for k in range(KB)], 0).astype(jnp.int32)
    column = lax.broadcasted_iota(jnp.int32, step.shape, 1)
    turn = (step * column) & (SG - 1)
    angle = turn.astype(F32) * F32(2.0 * math.pi / SG)
    cos, sin = jnp.cos(angle) * F32(1.0 / 256.0), jnp.sin(angle) * F32(1.0 / 256.0)
    rows = []
    for k in range(KB):
        c, s = cos[k * groups : (k + 1) * groups], sin[k * groups : (k + 1) * groups]
        rows += [jnp.concatenate([c, s], 1), jnp.concatenate([-s, c], 1)]
    table = jnp.concatenate(rows, 0)
    high = table.astype(BF)
    e_ref[: table.shape[0], :] = high
    e_ref[table.shape[0] :, :] = (table - high.astype(F32)).astype(BF)


def slot_grid(ref, k, slot, groups, rows_v):
    real = ref[k, slot * rows_v : (slot + 1) * rows_v, :]
    imag = ref[k, (groups + slot) * rows_v : (groups + slot + 1) * rows_v, :]
    return jnp.concatenate([real, imag], 0)


def expand(wu_ref, fine_index):
    rows = weight_rows(fine_index, wu_ref.shape[0])
    for n in range(0, len(rows), 2):
        wu_ref[n * KS : (n + 2) * KS, :] = jnp.concatenate(rows[n : n + 2], 0).astype(BF)


def forward_kernel(at_ref, y_ref, d_ref, tc_ref, ts_ref, e_ref, *refs):
    meta_refs = refs[:-4]
    part_ref, ys_ref, gs_ref, wu_ref = refs[-4:]
    groups = 2 * len(meta_refs)
    d_table = d_ref[at_ref[0]]
    pieces = y_ref.shape[0]
    half = e_ref.shape[0] // 2
    band = half // KB
    rows_v = gs_ref.shape[1] // band
    lines = pieces // rows_v
    for k in range(KB):
        ys_ref[k] = y_ref[:, k * RES : (k + 1) * RES].astype(F32)
    for v in range(0, rows_v, BATCH):
        turned = []
        for n in range(BATCH):
            row = [ys_ref[k, pl.ds(v + n, lines, stride=rows_v), :] for k in range(KB)]
            row = jnp.concatenate(row, 1).astype(BF)
            spread = dot(d_table, jnp.concatenate([row, row], 0), ((1,), (0,)))
            spread = spread.reshape(RES // SUB, 2, SUB, SG)
            real_g, imag_g = spread[:, 0], spread[:, 1]
            cos = tc_ref[...].reshape(RES // SUB, SUB, SG)
            sin = ts_ref[...].reshape(RES // SUB, SUB, SG)
            real_h = (real_g * cos + imag_g * sin).reshape(RES, SG).astype(BF)
            imag_h = (imag_g * cos - real_g * sin).reshape(RES, SG).astype(BF)
            turned.append(jnp.concatenate([real_h, imag_h], 1))
        share = dot(e_ref[...], jnp.concatenate(turned, 0), ((1,), (1,)))
        share = share[:half] + share[half:]
        for n in range(BATCH):
            for k in range(KB):
                gs_ref[k, pl.ds(v + n, band, stride=rows_v), :] = share[
                    k * band : (k + 1) * band, n * RES : (n + 1) * RES
                ]
    for s in range(groups):
        grid = [slot_grid(gs_ref, k, s, groups, rows_v) for k in range(KB)]
        grid = jnp.concatenate(grid, 1)
        high = grid.astype(BF)
        low = (grid - high.astype(F32)).astype(BF)
        meta, start = slot_rows(meta_refs, s)
        expand(wu_ref.at[s], meta[start : start + 1, :])
        along = dot(jnp.concatenate([high, low], 0), wu_ref[s], ((1,), (0,)))
        along = along[: 2 * rows_v] + along[2 * rows_v :]
        wv = weights(meta[start + 1 : start + 2, :], rows_v)
        real = jnp.sum(along[:rows_v] * wv, 0, keepdims=True)
        imag = jnp.sum(along[rows_v:] * wv, 0, keepdims=True)
        place = slot_place(at_ref[0], s, groups)
        both = jnp.concatenate([real, imag], 0).astype(BF)
        for n in range(groups):
            part_ref[n, place] = both


def backward_kernel(at_ref, part_ref, e_ref, tc_ref, ts_ref, d_ref, *refs):
    meta_refs = refs[:-8]
    res_ref, out_ref, pred_ref, rs_ref, im_ref, wu_ref, ct_ref, m_ref = refs[-8:]
    groups = 2 * len(meta_refs)
    slots = res_ref.shape[2]
    d_table = d_ref[at_ref[0]]
    lines = d_table.shape[0]
    band = 2 * groups
    rows_v = rs_ref.shape[1] // band
    pred_ref[...] = jnp.sum(part_ref[...].astype(F32), 0)
    slot = lax.broadcasted_iota(jnp.int32, (2, slots), 1).astype(F32)
    for s in range(groups):
        place = slot_place(at_ref[0], s, groups)
        meta, start = slot_rows(meta_refs, s)
        seen = meta[start + 2 : start + 4, :] - pred_ref[place]
        residual = jnp.where(slot < meta[start + 5 : start + 6, :], seen, F32(0.0))
        if s == 0:
            res_ref[0] = residual[0:1]
            res_ref[1] = residual[1:2]
        wv = weights(meta[start + 1 : start + 2, :], rows_v)
        spread = jnp.concatenate([wv * residual[0:1], wv * residual[1:2]], 0).astype(BF)
        expand(wu_ref.at[s], meta[start : start + 1, :])
        cells = dot(spread, wu_ref[s], ((1,), (1,)))
        for k in range(KB):
            part = cells[:, k * RES : (k + 1) * RES]
            rs_ref[k, s * rows_v : (s + 1) * rows_v, :] = part[:rows_v]
            rs_ref[k, (groups + s) * rows_v : (groups + s + 1) * rows_v, :] = part[rows_v:]
    for v in range(rows_v):
        rows = [rs_ref[k, pl.ds(v, band, stride=rows_v), :] for k in range(KB)]
        ct_ref[v] = jnp.concatenate(rows, 0).T.astype(BF)
    e_table = e_ref[: KB * band, :]

    def turn_chunk(wave, f):
        v = wave * WAVE
        cos = tc_ref[f : f + CHUNK, :]
        sin = ts_ref[f : f + CHUNK, :]
        cells = ct_ref[v : v + WAVE, f : f + CHUNK, :].reshape(WAVE * CHUNK, KB * band)
        back = dot(cells, e_table, ((1,), (0,))).reshape(WAVE, CHUNK, 2 * SG)
        real_b, imag_b = back[..., :SG], back[..., SG:]
        m_ref[v : v + WAVE, f : f + CHUNK, :] = (real_b * cos - imag_b * sin).astype(BF)
        m_ref[v : v + WAVE, RES + f : RES + f + CHUNK, :] = (
            imag_b * cos + real_b * sin
        ).astype(BF)

    def make_block(v):
        image = dot(d_table, m_ref[v], ((1,), (0,)))
        for k in range(KB):
            im_ref[k, pl.ds(v, lines, stride=rows_v), :] = image[:, k * RES : (k + 1) * RES]

    for n in range(0, RES, CHUNK):
        for wave in range(rows_v // WAVE):
            turn_chunk(wave, n)
    for v in range(rows_v):
        make_block(v)
    for k in range(KB):
        out_ref[:, k * RES : (k + 1) * RES] = im_ref[k].astype(BF)


def shards(facet_data, subgrid_pos, vis_counts, vis_u_fine, vis_v_fine, vis_observed):
    facets = lax.axis_size("facet")
    subs = lax.axis_size("sub")
    rows_v = facet_data.shape[1]
    slots = vis_u_fine.shape[1]
    facet = lax.axis_index("facet")

    params = pltpu.CompilerParams(vmem_limit_bytes=24 * 1024 * 1024)
    vmem = pl.BlockSpec(memory_space=pltpu.VMEM)
    smem = pl.BlockSpec(memory_space=pltpu.SMEM)
    hbm = pl.BlockSpec(memory_space=pltpu.HBM)
    copies, meta = pl.pallas_call(
        lead_kernel,
        out_shape=(
            jax.ShapeDtypeStruct((subs,) + facet_data.shape, BF),
            jax.ShapeDtypeStruct((ROWS, slots), F32),
        ),
        in_specs=[smem] * 2 + [hbm] * 4,
        out_specs=(hbm, vmem),
        scratch_shapes=[
            pltpu.VMEM(facet_data.shape, BF),
            pltpu.VMEM((1, slots), jnp.int32),
            pltpu.VMEM((1, slots), jnp.int32),
            pltpu.VMEM((2, 1, slots), F32),
            pltpu.SemaphoreType.DMA((4,)),
            pltpu.SemaphoreType.DMA((subs,)),
        ],
        compiler_params=params,
        name="lead",
    )(
        subgrid_pos, vis_counts,
        *(
            pltpu.with_memory_space_constraint(value, pltpu.HBM)
            for value in (facet_data, vis_u_fine, vis_v_fine, vis_observed)
        ),
    )
    gathered = lax.all_to_all(copies, "sub", 0, 0, tiled=True)

    table = block_tables(facets, subs)
    high_d, low_d = host_split(table)
    into = np.concatenate([high_d, low_d], 2)
    into = into.reshape(facets, 2, RES // SUB, SUB, -1).swapaxes(1, 2)
    into = jnp.asarray(into.reshape(facets, 2 * RES, -1))
    outof = jnp.asarray(high_d.transpose(0, 2, 1))
    turn = np.arange(RES)[:, None] * np.arange(SG)[None, :] * (2.0 * math.pi / 65536)
    tw_cos = jnp.asarray(np.cos(turn).astype(np.float32))
    tw_sin = jnp.asarray(np.sin(turn).astype(np.float32))
    partner = lax.ppermute(meta, "facet", [(n, n ^ 1) for n in range(facets)])
    pairs = [jnp.concatenate([meta, partner], 0)]
    for d in range(2, facets, 2):
        ring = [(n, (n + d) % facets) for n in range(facets)]
        pairs.append(lax.ppermute(pairs[0], "facet", ring))

    e_table = pl.pallas_call(
        table_kernel,
        out_shape=jax.ShapeDtypeStruct((4 * KB * facets, 2 * SG), BF),
        in_specs=[vmem] * (3 + facets // 2),
        out_specs=vmem,
        compiler_params=params,
        name="position_table",
    )(*pairs, into, tw_cos, tw_sin)

    at = facet.astype(jnp.int32)[None]
    part = pl.pallas_call(
        forward_kernel,
        out_shape=jax.ShapeDtypeStruct((facets, facets, 2, slots), BF),
        in_specs=[smem] + [vmem] * (5 + facets // 2),
        scratch_shapes=[
            pltpu.VMEM((KB, 2 * subs * rows_v, RES), F32),
            pltpu.VMEM((KB, 2 * facets * rows_v, RES), F32),
            pltpu.VMEM((facets, SG, slots), BF),
        ],
        compiler_params=params,
        name="forward_share",
    )(
        at, gathered.reshape(2 * subs * rows_v, SG), into, tw_cos, tw_sin, e_table,
        *pairs,
    )

    parts = lax.all_to_all(part, "facet", 0, 0, tiled=True)

    residual, image = pl.pallas_call(
        backward_kernel,
        out_shape=(
            jax.ShapeDtypeStruct((2, 1, slots), F32),
            jax.ShapeDtypeStruct((2 * subs * rows_v, SG), BF),
        ),
        in_specs=[smem] + [vmem] * (5 + facets // 2),
        scratch_shapes=[
            pltpu.VMEM((facets, 2, slots), F32),
            pltpu.VMEM((KB, 2 * facets * rows_v, RES), F32),
            pltpu.VMEM((KB, 2 * subs * rows_v, RES), F32),
            pltpu.VMEM((facets, SG, slots), BF),
            pltpu.VMEM((rows_v, RES, 2 * KB * facets), BF),
            pltpu.VMEM((rows_v, 2 * RES, SG), BF),
        ],
        compiler_params=params,
        name="backward_share",
    )(at, parts, e_table, tw_cos, tw_sin, outof, *pairs)

    image = image.reshape(subs, 2, rows_v, SG)
    image = lax.all_to_all(image, "sub", 0, 0, tiled=True)
    return (residual, jnp.sum(image.astype(F32), 0))


def solution(mesh):
    return jax.shard_map(
        shards,
        mesh=mesh,
        in_specs=(
            P(None, None, ("facet", "sub")),
            P(("facet", "sub")),
            P(("facet", "sub")),
            P(("facet", "sub"), None),
            P(("facet", "sub"), None),
            P(None, ("facet", "sub"), None),
        ),
        out_specs=(P(None, ("facet", "sub"), None), P(None, None, ("facet", "sub"))),
        check_vma=False,
    )
```

```python
import math

import jax
import jax.numpy as jnp
import numpy as np
from jax import lax
from jax.experimental import pallas as pl
from jax.experimental.pallas import tpu as pltpu
from jax.sharding import PartitionSpec as P

SG = 512
KS = 8
OVER = 16
RES = 128
KB = SG // RES
BATCH = 4
CHUNK = 16
WAVE = 16
SUB = 8
ROWS = 8
BF = jnp.bfloat16
F32 = jnp.float32


def block_tables(facets, subs):
    block = np.arange(facets * subs).reshape(facets, subs)
    turn = (np.arange(RES)[None, :, None] * block[:, None, :]) % RES
    angle = turn * (2.0 * math.pi / RES)
    cos, sin = np.cos(angle), np.sin(angle)
    top = np.stack([cos, sin], -1)
    low = np.stack([-sin, cos], -1)
    table = np.concatenate([top, low], 1).reshape(facets, 2 * RES, 2 * subs)
    return table.astype(np.float32)


def host_split(table):
    high = table.astype(jnp.bfloat16)
    return high, (table - high.astype(np.float32)).astype(jnp.bfloat16)


def weights(fine_index, cells):
    middle = fine_index / OVER + (KS - 1) / 2.0
    cell = jnp.floor(fine_index / OVER)
    row = lax.broadcasted_iota(jnp.int32, (cells, fine_index.shape[1]), 0).astype(F32)
    distance = (row - middle) / 0.6
    weight = jnp.exp(-0.5 * (distance * distance))
    return jnp.where((row >= cell) & (row < cell + KS), weight, F32(0.0))


def weight_rows(fine_index, cells):
    cell = jnp.floor(fine_index / OVER)
    tile = jnp.floor(cell / KS)
    inner = cell - tile * KS
    row = lax.broadcasted_iota(jnp.int32, (KS, fine_index.shape[1]), 0).astype(F32)
    wrapped = row < inner
    offset = row - inner + jnp.where(wrapped, F32(KS), F32(0.0))
    distance = (offset - ((KS - 1) / 2.0 + (fine_index / OVER - cell))) / 0.6
    weight = jnp.exp(-0.5 * (distance * distance))
    tile = tile + jnp.where(wrapped, F32(1.0), F32(0.0))
    return [jnp.where(tile == F32(n), weight, F32(0.0)) for n in range(cells // KS)]


def dot(left, right, dims):
    return lax.dot_general(left, right, (dims, ((), ())), preferred_element_type=F32)


def slot_rows(refs, slot):
    start = (slot % 2) * ROWS
    return refs[slot // 2], start


def slot_place(at, slot, groups):
    return ((at - (slot // 2) * 2) & (groups - 1)) ^ (slot % 2)


def lead_kernel(
    pos_ref, cnt_ref, y_hbm, u_hbm, v_hbm, obs_hbm, copy_hbm, meta_ref,
    y_ref, u_ref, v_ref, obs_ref, load_sem, send_sem,
):
    slots = u_ref.shape[1]
    pairs = [(y_hbm, y_ref), (u_hbm, u_ref), (v_hbm, v_ref), (obs_hbm, obs_ref)]
    loads = [
        pltpu.make_async_copy(source, target, load_sem.at[n])
        for n, (source, target) in enumerate(pairs)
    ]
    for load in loads:
        load.start()
    loads[0].wait()
    sends = [
        pltpu.make_async_copy(y_ref, copy_hbm.at[n], send_sem.at[n])
        for n in range(copy_hbm.shape[0])
    ]
    for send in sends:
        send.start()
    for load in loads[1:]:
        load.wait()
    meta_ref[0:1, :] = u_ref[...].astype(F32)
    meta_ref[1:2, :] = v_ref[...].astype(F32)
    meta_ref[2:3, :] = obs_ref[0]
    meta_ref[3:4, :] = obs_ref[1]
    meta_ref[4:5, :] = jnp.full((1, slots), pos_ref[0] // RES, jnp.int32).astype(F32)
    meta_ref[5:6, :] = jnp.full((1, slots), cnt_ref[0], jnp.int32).astype(F32)
    meta_ref[6:8, :] = jnp.zeros((2, slots), F32)
    for send in sends:
        send.wait()


def interleave(real, imag):
    parts = []
    for n in range(0, real.shape[1], RES):
        parts += [real[:, n : n + RES], imag[:, n : n + RES]]
    return jnp.concatenate(parts, 1)


def table_kernel(*refs):
    e_ref = refs[-1]
    pairs = refs[: len(refs) - 4]
    groups = 2 * len(pairs)
    spot = jnp.concatenate([p[n : n + 1, :] for p in pairs for n in (4, 4 + ROWS)], 0)
    step = jnp.concatenate([spot + F32(k) for k in range(KB)], 0).astype(jnp.int32)
    column = lax.broadcasted_iota(jnp.int32, step.shape, 1)
    turn = (step * column) & (SG - 1)
    angle = turn.astype(F32) * F32(2.0 * math.pi / SG)
    cos, sin = jnp.cos(angle) * F32(1.0 / 256.0), jnp.sin(angle) * F32(1.0 / 256.0)
    rows = []
    for k in range(KB):
        c, s = cos[k * groups : (k + 1) * groups], sin[k * groups : (k + 1) * groups]
        rows += [interleave(c, s), interleave(-s, c)]
    table = jnp.concatenate(rows, 0)
    high = table.astype(BF)
    e_ref[: table.shape[0], :] = high
    e_ref[table.shape[0] :, :] = (table - high.astype(F32)).astype(BF)


def slot_grid(ref, k, slot, groups, rows_v):
    real = ref[k, slot * rows_v : (slot + 1) * rows_v, :]
    imag = ref[k, (groups + slot) * rows_v : (groups + slot + 1) * rows_v, :]
    return jnp.concatenate([real, imag], 0)


def expand(wu_ref, fine_index):
    rows = weight_rows(fine_index, wu_ref.shape[0])
    for n in range(0, len(rows), 2):
        wu_ref[n * KS : (n + 2) * KS, :] = jnp.concatenate(rows[n : n + 2], 0).astype(BF)


def forward_kernel(y_ref, d_ref, tc_ref, ts_ref, e_ref, *refs):
    meta_refs = refs[:-4]
    part_ref, ys_ref, gs_ref, wu_ref = refs[-4:]
    groups = 2 * len(meta_refs)
    at = lax.axis_index("facet")
    d_table = d_ref[at]
    pieces = y_ref.shape[0]
    half = e_ref.shape[0] // 2
    band = half // KB
    rows_v = gs_ref.shape[1] // band
    lines = pieces // rows_v
    for k in range(KB):
        ys_ref[k] = y_ref[:, k * RES : (k + 1) * RES].astype(F32)
    for v in range(0, rows_v, BATCH):
        turned = []
        for n in range(BATCH):
            row = [ys_ref[k, pl.ds(v + n, lines, stride=rows_v), :] for k in range(KB)]
            row = jnp.concatenate(row, 1).astype(BF)
            spread = dot(d_table, jnp.concatenate([row, row], 0), ((1,), (0,)))
            spread = spread.reshape(RES // SUB, 2, SUB, SG)
            real_g, imag_g = spread[:, 0], spread[:, 1]
            cos = tc_ref[...].reshape(RES // SUB, SUB, SG)
            sin = ts_ref[...].reshape(RES // SUB, SUB, SG)
            real_h = (real_g * cos + imag_g * sin).reshape(RES, SG).astype(BF)
            imag_h = (imag_g * cos - real_g * sin).reshape(RES, SG).astype(BF)
            turned.append(interleave(real_h, imag_h))
        share = dot(e_ref[...], jnp.concatenate(turned, 0), ((1,), (1,)))
        share = share[:half] + share[half:]
        for n in range(BATCH):
            for k in range(KB):
                gs_ref[k, pl.ds(v + n, band, stride=rows_v), :] = share[
                    k * band : (k + 1) * band, n * RES : (n + 1) * RES
                ]
    for s in range(groups):
        grid = [slot_grid(gs_ref, k, s, groups, rows_v) for k in range(KB)]
        grid = jnp.concatenate(grid, 1)
        high = grid.astype(BF)
        low = (grid - high.astype(F32)).astype(BF)
        meta, start = slot_rows(meta_refs, s)
        expand(wu_ref.at[s], meta[start : start + 1, :])
        along = dot(jnp.concatenate([high, low], 0), wu_ref[s], ((1,), (0,)))
        along = along[: 2 * rows_v] + along[2 * rows_v :]
        wv = weights(meta[start + 1 : start + 2, :], rows_v)
        real = jnp.sum(along[:rows_v] * wv, 0, keepdims=True)
        imag = jnp.sum(along[rows_v:] * wv, 0, keepdims=True)
        place = slot_place(at, s, groups)
        both = jnp.concatenate([real, imag], 0).astype(BF)
        for n in range(groups):
            part_ref[n, place] = both


def backward_kernel(part_ref, e_ref, tc_ref, ts_ref, d_ref, *refs):
    meta_refs = refs[:-10]
    res_hbm, out_ref, pred_ref, rs_ref, im_ref, wu_ref, ct_ref, m_ref, res_ref, sem = refs[-10:]
    groups = 2 * len(meta_refs)
    slots = res_ref.shape[2]
    store = pltpu.make_async_copy(res_ref, res_hbm, sem)
    at = lax.axis_index("facet")
    d_table = d_ref[at]
    lines = d_table.shape[0]
    band = 2 * groups
    rows_v = rs_ref.shape[1] // band
    pred_ref[...] = jnp.sum(part_ref[...].astype(F32), 0)
    slot = lax.broadcasted_iota(jnp.int32, (2, slots), 1).astype(F32)
    for s in range(groups):
        place = slot_place(at, s, groups)
        meta, start = slot_rows(meta_refs, s)
        seen = meta[start + 2 : start + 4, :] - pred_ref[place]
        residual = jnp.where(slot < meta[start + 5 : start + 6, :], seen, F32(0.0))
        if s == 0:
            res_ref[0] = residual[0:1]
            res_ref[1] = residual[1:2]
            store.start()
        wv = weights(meta[start + 1 : start + 2, :], rows_v)
        spread = jnp.concatenate([wv * residual[0:1], wv * residual[1:2]], 0).astype(BF)
        expand(wu_ref.at[s], meta[start : start + 1, :])
        cells = dot(spread, wu_ref[s], ((1,), (1,)))
        for k in range(KB):
            part = cells[:, k * RES : (k + 1) * RES]
            rs_ref[k, s * rows_v : (s + 1) * rows_v, :] = part[:rows_v]
            rs_ref[k, (groups + s) * rows_v : (groups + s + 1) * rows_v, :] = part[rows_v:]
    for v in range(rows_v):
        rows = [rs_ref[k, pl.ds(v, band, stride=rows_v), :] for k in range(KB)]
        ct_ref[v] = jnp.concatenate(rows, 0).T.astype(BF)

    def turn_chunk(wave, f):
        v = wave * WAVE
        cells = ct_ref[v : v + WAVE, f : f + CHUNK, :].reshape(WAVE * CHUNK, KB * band)
        for n in range(0, SG, RES):
            cos = tc_ref[f : f + CHUNK, n : n + RES]
            sin = ts_ref[f : f + CHUNK, n : n + RES]
            back = dot(cells, e_ref[: KB * band, 2 * n : 2 * (n + RES)], ((1,), (0,)))
            back = back.reshape(WAVE, CHUNK, 2 * RES)
            real_b, imag_b = back[..., :RES], back[..., RES:]
            m_ref[v : v + WAVE, f : f + CHUNK, n : n + RES] = (
                real_b * cos - imag_b * sin
            ).astype(BF)
            m_ref[v : v + WAVE, RES + f : RES + f + CHUNK, n : n + RES] = (
                imag_b * cos + real_b * sin
            ).astype(BF)

    def make_block(v):
        image = dot(d_table, m_ref[v], ((1,), (0,)))
        for k in range(KB):
            im_ref[k, pl.ds(v, lines, stride=rows_v), :] = image[:, k * RES : (k + 1) * RES]

    for n in range(0, RES, CHUNK):
        for wave in range(rows_v // WAVE):
            turn_chunk(wave, n)
    for v in range(rows_v):
        make_block(v)
    for k in range(KB):
        out_ref[:, k * RES : (k + 1) * RES] = im_ref[k].astype(BF)
    store.wait()


def shards(facet_data, subgrid_pos, vis_counts, vis_u_fine, vis_v_fine, vis_observed):
    facets = lax.axis_size("facet")
    subs = lax.axis_size("sub")
    rows_v = facet_data.shape[1]
    slots = vis_u_fine.shape[1]

    params = pltpu.CompilerParams(vmem_limit_bytes=24 * 1024 * 1024)
    vmem = pl.BlockSpec(memory_space=pltpu.VMEM)
    hbm = pl.BlockSpec(memory_space=pltpu.HBM)
    smem = pl.BlockSpec(memory_space=pltpu.SMEM)
    copies, meta = pl.pallas_call(
        lead_kernel,
        out_shape=(
            jax.ShapeDtypeStruct((subs,) + facet_data.shape, BF),
            jax.ShapeDtypeStruct((ROWS, slots), F32),
        ),
        in_specs=[smem] * 2 + [hbm] * 4,
        out_specs=(hbm, vmem),
        scratch_shapes=[
            pltpu.VMEM(facet_data.shape, BF),
            pltpu.VMEM((1, slots), jnp.int32),
            pltpu.VMEM((1, slots), jnp.int32),
            pltpu.VMEM((2, 1, slots), F32),
            pltpu.SemaphoreType.DMA((4,)),
            pltpu.SemaphoreType.DMA((subs,)),
        ],
        compiler_params=params,
        name="lead",
    )(
        subgrid_pos, vis_counts,
        *(
            pltpu.with_memory_space_constraint(value, pltpu.HBM)
            for value in (facet_data, vis_u_fine, vis_v_fine, vis_observed)
        ),
    )
    gathered = lax.all_to_all(copies, "sub", 0, 0, tiled=True)

    table = block_tables(facets, subs)
    high_d, low_d = host_split(table)
    into = np.concatenate([high_d, low_d], 2)
    into = into.reshape(facets, 2, RES // SUB, SUB, -1).swapaxes(1, 2)
    into = jnp.asarray(into.reshape(facets, 2 * RES, -1))
    outof = jnp.asarray(high_d.transpose(0, 2, 1))
    turn = np.arange(RES)[:, None] * np.arange(SG)[None, :] * (2.0 * math.pi / 65536)
    tw_cos = jnp.asarray(np.cos(turn).astype(np.float32))
    tw_sin = jnp.asarray(np.sin(turn).astype(np.float32))
    partner = lax.ppermute(meta, "facet", [(n, n ^ 1) for n in range(facets)])
    pairs = [jnp.concatenate([meta, partner], 0)]
    for d in range(2, facets, 2):
        ring = [(n, (n + d) % facets) for n in range(facets)]
        pairs.append(lax.ppermute(pairs[0], "facet", ring))

    e_table = pl.pallas_call(
        table_kernel,
        out_shape=jax.ShapeDtypeStruct((4 * KB * facets, 2 * SG), BF),
        in_specs=[vmem] * (3 + facets // 2),
        out_specs=vmem,
        compiler_params=params,
        name="position_table",
    )(*pairs, into, tw_cos, tw_sin)

    part = pl.pallas_call(
        forward_kernel,
        out_shape=jax.ShapeDtypeStruct((facets, facets, 2, slots), BF),
        in_specs=[vmem] * (5 + facets // 2),
        scratch_shapes=[
            pltpu.VMEM((KB, 2 * subs * rows_v, RES), F32),
            pltpu.VMEM((KB, 2 * facets * rows_v, RES), F32),
            pltpu.VMEM((facets, SG, slots), BF),
        ],
        compiler_params=params,
        name="forward_share",
    )(
        gathered.reshape(2 * subs * rows_v, SG), into, tw_cos, tw_sin, e_table,
        *pairs,
    )

    parts = lax.all_to_all(part, "facet", 0, 0, tiled=True)

    residual, image = pl.pallas_call(
        backward_kernel,
        out_shape=(
            jax.ShapeDtypeStruct((2, 1, slots), F32),
            jax.ShapeDtypeStruct((2 * subs * rows_v, SG), BF),
        ),
        in_specs=[vmem] * (5 + facets // 2),
        scratch_shapes=[
            pltpu.VMEM((facets, 2, slots), F32),
            pltpu.VMEM((KB, 2 * facets * rows_v, RES), F32),
            pltpu.VMEM((KB, 2 * subs * rows_v, RES), F32),
            pltpu.VMEM((facets, SG, slots), BF),
            pltpu.VMEM((rows_v, RES, 2 * KB * facets), BF),
            pltpu.VMEM((rows_v, 2 * RES, SG), BF),
            pltpu.VMEM((2, 1, slots), F32),
            pltpu.SemaphoreType.DMA(()),
        ],
        out_specs=(hbm, vmem),
        compiler_params=params,
        name="backward_share",
    )(parts, e_table, tw_cos, tw_sin, outof, *pairs)

    image = image.reshape(subs, 2, rows_v, SG)
    image = lax.all_to_all(image, "sub", 0, 0, tiled=True)
    return (residual, jnp.sum(image.astype(F32), 0))


def solution(mesh):
    return jax.shard_map(
        shards,
        mesh=mesh,
        in_specs=(
            P(None, None, ("facet", "sub")),
            P(("facet", "sub")),
            P(("facet", "sub")),
            P(("facet", "sub"), None),
            P(("facet", "sub"), None),
            P(None, ("facet", "sub"), None),
        ),
        out_specs=(P(None, ("facet", "sub"), None), P(None, None, ("facet", "sub"))),
        check_vma=False,
    )
```

```python
import math

import jax
import jax.numpy as jnp
import numpy as np
from jax import lax
from jax.experimental import pallas as pl
from jax.experimental.pallas import tpu as pltpu
from jax.sharding import PartitionSpec as P

SG = 512
KS = 8
OVER = 16
RES = 128
KB = SG // RES
BATCH = 4
CHUNK = 16
WAVE = 8
SUB = 8
ROWS = 8
BF = jnp.bfloat16
F32 = jnp.float32


def block_tables(facets, subs):
    block = np.arange(facets * subs).reshape(facets, subs)
    turn = (np.arange(RES)[None, :, None] * block[:, None, :]) % RES
    angle = turn * (2.0 * math.pi / RES)
    cos, sin = np.cos(angle), np.sin(angle)
    top = np.stack([cos, sin], -1)
    low = np.stack([-sin, cos], -1)
    table = np.concatenate([top, low], 1).reshape(facets, 2 * RES, 2 * subs)
    return table.astype(np.float32)


def host_split(table):
    high = table.astype(jnp.bfloat16)
    return high, (table - high.astype(np.float32)).astype(jnp.bfloat16)


def weights(fine_index, cells):
    middle = fine_index / OVER + (KS - 1) / 2.0
    cell = jnp.floor(fine_index / OVER)
    row = lax.broadcasted_iota(jnp.int32, (cells, fine_index.shape[1]), 0).astype(F32)
    distance = (row - middle) / 0.6
    weight = jnp.exp(-0.5 * (distance * distance))
    return jnp.where((row >= cell) & (row < cell + KS), weight, F32(0.0))


def weight_rows(fine_index, cells):
    cell = jnp.floor(fine_index / OVER)
    tile = jnp.floor(cell / KS)
    inner = cell - tile * KS
    row = lax.broadcasted_iota(jnp.int32, (KS, fine_index.shape[1]), 0).astype(F32)
    wrapped = row < inner
    offset = row - inner + jnp.where(wrapped, F32(KS), F32(0.0))
    distance = (offset - ((KS - 1) / 2.0 + (fine_index / OVER - cell))) / 0.6
    weight = jnp.exp(-0.5 * (distance * distance))
    tile = tile + jnp.where(wrapped, F32(1.0), F32(0.0))
    return [jnp.where(tile == F32(n), weight, F32(0.0)) for n in range(cells // KS)]


def dot(left, right, dims):
    return lax.dot_general(left, right, (dims, ((), ())), preferred_element_type=F32)


def slot_rows(refs, slot):
    start = (slot % 2) * ROWS
    return refs[slot // 2], start


def slot_place(at, slot, groups):
    return ((at - (slot // 2) * 2) & (groups - 1)) ^ (slot % 2)


def lead_kernel(
    pos_ref, cnt_ref, y_hbm, u_hbm, v_hbm, obs_hbm, copy_hbm, meta_ref,
    y_ref, u_ref, v_ref, obs_ref, load_sem, send_sem,
):
    slots = u_ref.shape[1]
    pairs = [(y_hbm, y_ref), (u_hbm, u_ref), (v_hbm, v_ref), (obs_hbm, obs_ref)]
    loads = [
        pltpu.make_async_copy(source, target, load_sem.at[n])
        for n, (source, target) in enumerate(pairs)
    ]
    for load in loads:
        load.start()
    loads[0].wait()
    sends = [
        pltpu.make_async_copy(y_ref, copy_hbm.at[n], send_sem.at[n])
        for n in range(copy_hbm.shape[0])
    ]
    for send in sends:
        send.start()
    for load in loads[1:]:
        load.wait()
    meta_ref[0:1, :] = u_ref[...].astype(F32)
    meta_ref[1:2, :] = v_ref[...].astype(F32)
    meta_ref[2:3, :] = obs_ref[0]
    meta_ref[3:4, :] = obs_ref[1]
    meta_ref[4:5, :] = jnp.full((1, slots), pos_ref[0] // RES, jnp.int32).astype(F32)
    meta_ref[5:6, :] = jnp.full((1, slots), cnt_ref[0], jnp.int32).astype(F32)
    meta_ref[6:8, :] = jnp.zeros((2, slots), F32)
    for send in sends:
        send.wait()


def interleave(real, imag):
    parts = []
    for n in range(0, real.shape[1], RES):
        parts += [real[:, n : n + RES], imag[:, n : n + RES]]
    return jnp.concatenate(parts, 1)


def table_kernel(*refs):
    e_ref = refs[-1]
    pairs = refs[: len(refs) - 4]
    groups = 2 * len(pairs)
    spot = jnp.concatenate([p[n : n + 1, :] for p in pairs for n in (4, 4 + ROWS)], 0)
    step = jnp.concatenate([spot + F32(k) for k in range(KB)], 0).astype(jnp.int32)
    column = lax.broadcasted_iota(jnp.int32, step.shape, 1)
    turn = (step * column) & (SG - 1)
    angle = turn.astype(F32) * F32(2.0 * math.pi / SG)
    cos, sin = jnp.cos(angle) * F32(1.0 / 256.0), jnp.sin(angle) * F32(1.0 / 256.0)
    rows = []
    for k in range(KB):
        c, s = cos[k * groups : (k + 1) * groups], sin[k * groups : (k + 1) * groups]
        rows += [interleave(c, s), interleave(-s, c)]
    table = jnp.concatenate(rows, 0)
    high = table.astype(BF)
    e_ref[: table.shape[0], :] = high
    e_ref[table.shape[0] :, :] = (table - high.astype(F32)).astype(BF)


def slot_grid(ref, k, slot, groups, rows_v):
    real = ref[k, slot * rows_v : (slot + 1) * rows_v, :]
    imag = ref[k, (groups + slot) * rows_v : (groups + slot + 1) * rows_v, :]
    return jnp.concatenate([real, imag], 0)


def expand(wu_ref, fine_index):
    rows = weight_rows(fine_index, wu_ref.shape[0])
    for n in range(0, len(rows), 2):
        wu_ref[n * KS : (n + 2) * KS, :] = jnp.concatenate(rows[n : n + 2], 0).astype(BF)


def forward_kernel(y_ref, d_ref, tc_ref, ts_ref, e_ref, *refs):
    meta_refs = refs[:-4]
    part_ref, ys_ref, gs_ref, wu_ref = refs[-4:]
    groups = 2 * len(meta_refs)
    at = lax.axis_index("facet")
    d_table = d_ref[at]
    pieces = y_ref.shape[0]
    half = e_ref.shape[0] // 2
    band = half // KB
    rows_v = gs_ref.shape[1] // band
    lines = pieces // rows_v
    for k in range(KB):
        ys_ref[k] = y_ref[:, k * RES : (k + 1) * RES].astype(F32)
    for v in range(0, rows_v, BATCH):
        turned = []
        for n in range(BATCH):
            row = [ys_ref[k, pl.ds(v + n, lines, stride=rows_v), :] for k in range(KB)]
            row = jnp.concatenate(row, 1).astype(BF)
            spread = dot(d_table, jnp.concatenate([row, row], 0), ((1,), (0,)))
            spread = spread.reshape(RES // SUB, 2, SUB, SG)
            real_g, imag_g = spread[:, 0], spread[:, 1]
            cos = tc_ref[...].reshape(RES // SUB, SUB, SG)
            sin = ts_ref[...].reshape(RES // SUB, SUB, SG)
            real_h = (real_g * cos + imag_g * sin).reshape(RES, SG).astype(BF)
            imag_h = (imag_g * cos - real_g * sin).reshape(RES, SG).astype(BF)
            turned.append(interleave(real_h, imag_h))
        share = dot(e_ref[...], jnp.concatenate(turned, 0), ((1,), (1,)))
        share = share[:half] + share[half:]
        for n in range(BATCH):
            for k in range(KB):
                gs_ref[k, pl.ds(v + n, band, stride=rows_v), :] = share[
                    k * band : (k + 1) * band, n * RES : (n + 1) * RES
                ]
    for s in range(groups):
        grid = [slot_grid(gs_ref, k, s, groups, rows_v) for k in range(KB)]
        grid = jnp.concatenate(grid, 1)
        high = grid.astype(BF)
        low = (grid - high.astype(F32)).astype(BF)
        meta, start = slot_rows(meta_refs, s)
        expand(wu_ref.at[s], meta[start : start + 1, :])
        along = dot(jnp.concatenate([high, low], 0), wu_ref[s], ((1,), (0,)))
        along = along[: 2 * rows_v] + along[2 * rows_v :]
        wv = weights(meta[start + 1 : start + 2, :], rows_v)
        real = jnp.sum(along[:rows_v] * wv, 0, keepdims=True)
        imag = jnp.sum(along[rows_v:] * wv, 0, keepdims=True)
        place = slot_place(at, s, groups)
        both = jnp.concatenate([real, imag], 0).astype(BF)
        for n in range(groups):
            part_ref[n, place] = both


def backward_kernel(part_ref, e_ref, tc_ref, ts_ref, d_ref, *refs):
    meta_refs = refs[:-10]
    res_hbm, out_ref, pred_ref, rs_ref, im_ref, wu_ref, ct_ref, m_ref, res_ref, sem = refs[-10:]
    groups = 2 * len(meta_refs)
    slots = res_ref.shape[2]
    store = pltpu.make_async_copy(res_ref, res_hbm, sem)
    at = lax.axis_index("facet")
    d_table = d_ref[at]
    lines = d_table.shape[0]
    band = 2 * groups
    rows_v = rs_ref.shape[1] // band
    pred_ref[...] = jnp.sum(part_ref[...].astype(F32), 0)
    slot = lax.broadcasted_iota(jnp.int32, (2, slots), 1).astype(F32)
    for s in range(groups):
        place = slot_place(at, s, groups)
        meta, start = slot_rows(meta_refs, s)
        seen = meta[start + 2 : start + 4, :] - pred_ref[place]
        residual = jnp.where(slot < meta[start + 5 : start + 6, :], seen, F32(0.0))
        if s == 0:
            res_ref[0] = residual[0:1]
            res_ref[1] = residual[1:2]
            store.start()
        wv = weights(meta[start + 1 : start + 2, :], rows_v)
        spread = jnp.concatenate([wv * residual[0:1], wv * residual[1:2]], 0).astype(BF)
        expand(wu_ref.at[s], meta[start : start + 1, :])
        cells = dot(spread, wu_ref[s], ((1,), (1,)))
        for k in range(KB):
            part = cells[:, k * RES : (k + 1) * RES]
            rs_ref[k, s * rows_v : (s + 1) * rows_v, :] = part[:rows_v]
            rs_ref[k, (groups + s) * rows_v : (groups + s + 1) * rows_v, :] = part[rows_v:]
    for v in range(rows_v):
        rows = [rs_ref[k, pl.ds(v, band, stride=rows_v), :] for k in range(KB)]
        ct_ref[v] = jnp.concatenate(rows, 0).T.astype(BF)

    def turn_chunk(wave, f):
        v = wave * WAVE
        cells = ct_ref[v : v + WAVE, f : f + CHUNK, :].reshape(WAVE * CHUNK, KB * band)
        for n in range(0, SG, RES):
            cos = tc_ref[f : f + CHUNK, n : n + RES]
            sin = ts_ref[f : f + CHUNK, n : n + RES]
            back = dot(cells, e_ref[: KB * band, 2 * n : 2 * (n + RES)], ((1,), (0,)))
            back = back.reshape(WAVE, CHUNK, 2 * RES)
            real_b, imag_b = back[..., :RES], back[..., RES:]
            m_ref[v : v + WAVE, f : f + CHUNK, n : n + RES] = (
                real_b * cos - imag_b * sin
            ).astype(BF)
            m_ref[v : v + WAVE, RES + f : RES + f + CHUNK, n : n + RES] = (
                imag_b * cos + real_b * sin
            ).astype(BF)

    def make_block(v):
        image = dot(d_table, m_ref[v], ((1,), (0,)))
        for k in range(KB):
            im_ref[k, pl.ds(v, lines, stride=rows_v), :] = image[:, k * RES : (k + 1) * RES]

    waves = rows_v // WAVE
    steps = RES // CHUNK
    for wave in range(waves + 1):
        for n in range(steps):
            if wave < waves:
                turn_chunk(wave, n * CHUNK)
            if wave > 0:
                for v in range(n * WAVE // steps, (n + 1) * WAVE // steps):
                    make_block((wave - 1) * WAVE + v)
    for k in range(KB):
        out_ref[:, k * RES : (k + 1) * RES] = im_ref[k].astype(BF)
    store.wait()


def shards(facet_data, subgrid_pos, vis_counts, vis_u_fine, vis_v_fine, vis_observed):
    facets = lax.axis_size("facet")
    subs = lax.axis_size("sub")
    rows_v = facet_data.shape[1]
    slots = vis_u_fine.shape[1]

    params = pltpu.CompilerParams(vmem_limit_bytes=24 * 1024 * 1024)
    vmem = pl.BlockSpec(memory_space=pltpu.VMEM)
    hbm = pl.BlockSpec(memory_space=pltpu.HBM)
    smem = pl.BlockSpec(memory_space=pltpu.SMEM)
    copies, meta = pl.pallas_call(
        lead_kernel,
        out_shape=(
            jax.ShapeDtypeStruct((subs,) + facet_data.shape, BF),
            jax.ShapeDtypeStruct((ROWS, slots), F32),
        ),
        in_specs=[smem] * 2 + [hbm] * 4,
        out_specs=(hbm, vmem),
        scratch_shapes=[
            pltpu.VMEM(facet_data.shape, BF),
            pltpu.VMEM((1, slots), jnp.int32),
            pltpu.VMEM((1, slots), jnp.int32),
            pltpu.VMEM((2, 1, slots), F32),
            pltpu.SemaphoreType.DMA((4,)),
            pltpu.SemaphoreType.DMA((subs,)),
        ],
        compiler_params=params,
        name="lead",
    )(
        subgrid_pos, vis_counts,
        *(
            pltpu.with_memory_space_constraint(value, pltpu.HBM)
            for value in (facet_data, vis_u_fine, vis_v_fine, vis_observed)
        ),
    )
    gathered = lax.all_to_all(copies, "sub", 0, 0, tiled=True)

    table = block_tables(facets, subs)
    high_d, low_d = host_split(table)
    into = np.concatenate([high_d, low_d], 2)
    into = into.reshape(facets, 2, RES // SUB, SUB, -1).swapaxes(1, 2)
    into = jnp.asarray(into.reshape(facets, 2 * RES, -1))
    outof = jnp.asarray(high_d.transpose(0, 2, 1))
    turn = np.arange(RES)[:, None] * np.arange(SG)[None, :] * (2.0 * math.pi / 65536)
    tw_cos = jnp.asarray(np.cos(turn).astype(np.float32))
    tw_sin = jnp.asarray(np.sin(turn).astype(np.float32))
    partner = lax.ppermute(meta, "facet", [(n, n ^ 1) for n in range(facets)])
    pairs = [jnp.concatenate([meta, partner], 0)]
    for d in range(2, facets, 2):
        ring = [(n, (n + d) % facets) for n in range(facets)]
        pairs.append(lax.ppermute(pairs[0], "facet", ring))

    e_table = pl.pallas_call(
        table_kernel,
        out_shape=jax.ShapeDtypeStruct((4 * KB * facets, 2 * SG), BF),
        in_specs=[vmem] * (3 + facets // 2),
        out_specs=vmem,
        compiler_params=params,
        name="position_table",
    )(*pairs, into, tw_cos, tw_sin)

    part = pl.pallas_call(
        forward_kernel,
        out_shape=jax.ShapeDtypeStruct((facets, facets, 2, slots), BF),
        in_specs=[vmem] * (5 + facets // 2),
        scratch_shapes=[
            pltpu.VMEM((KB, 2 * subs * rows_v, RES), F32),
            pltpu.VMEM((KB, 2 * facets * rows_v, RES), F32),
            pltpu.VMEM((facets, SG, slots), BF),
        ],
        compiler_params=params,
        name="forward_share",
    )(
        gathered.reshape(2 * subs * rows_v, SG), into, tw_cos, tw_sin, e_table,
        *pairs,
    )

    parts = lax.all_to_all(part, "facet", 0, 0, tiled=True)

    residual, image = pl.pallas_call(
        backward_kernel,
        out_shape=(
            jax.ShapeDtypeStruct((2, 1, slots), F32),
            jax.ShapeDtypeStruct((2 * subs * rows_v, SG), BF),
        ),
        in_specs=[vmem] * (5 + facets // 2),
        scratch_shapes=[
            pltpu.VMEM((facets, 2, slots), F32),
            pltpu.VMEM((KB, 2 * facets * rows_v, RES), F32),
            pltpu.VMEM((KB, 2 * subs * rows_v, RES), F32),
            pltpu.VMEM((facets, SG, slots), BF),
            pltpu.VMEM((rows_v, RES, 2 * KB * facets), BF),
            pltpu.VMEM((rows_v, 2 * RES, SG), BF),
            pltpu.VMEM((2, 1, slots), F32),
            pltpu.SemaphoreType.DMA(()),
        ],
        out_specs=(hbm, vmem),
        compiler_params=params,
        name="backward_share",
    )(parts, e_table, tw_cos, tw_sin, outof, *pairs)

    image = image.reshape(subs, 2, rows_v, SG)
    image = lax.all_to_all(image, "sub", 0, 0, tiled=True)
    return (residual, jnp.sum(image.astype(F32), 0))


def solution(mesh):
    return jax.shard_map(
        shards,
        mesh=mesh,
        in_specs=(
            P(None, None, ("facet", "sub")),
            P(("facet", "sub")),
            P(("facet", "sub")),
            P(("facet", "sub"), None),
            P(("facet", "sub"), None),
            P(None, ("facet", "sub"), None),
        ),
        out_specs=(P(None, ("facet", "sub"), None), P(None, None, ("facet", "sub"))),
        check_vma=False,
    )
```

```python
import math

import jax
import jax.numpy as jnp
import numpy as np
from jax import lax
from jax.experimental import pallas as pl
from jax.experimental.pallas import tpu as pltpu
from jax.sharding import PartitionSpec as P

SG = 512
KS = 8
OVER = 16
RES = 128
KB = SG // RES
BATCH = 4
CHUNK = 16
WAVE = 8
SUB = 8
ROWS = 8
BF = jnp.bfloat16
F32 = jnp.float32


def block_tables(facets, subs):
    block = np.arange(facets * subs).reshape(facets, subs)
    turn = (np.arange(RES)[None, :, None] * block[:, None, :]) % RES
    angle = turn * (2.0 * math.pi / RES)
    cos, sin = np.cos(angle), np.sin(angle)
    top = np.stack([cos, sin], -1)
    low = np.stack([-sin, cos], -1)
    table = np.concatenate([top, low], 1).reshape(facets, 2 * RES, 2 * subs)
    return table.astype(np.float32)


def host_split(table):
    high = table.astype(jnp.bfloat16)
    return high, (table - high.astype(np.float32)).astype(jnp.bfloat16)


def weights(fine_index, cells):
    middle = fine_index / OVER + (KS - 1) / 2.0
    cell = jnp.floor(fine_index / OVER)
    row = lax.broadcasted_iota(jnp.int32, (cells, fine_index.shape[1]), 0).astype(F32)
    distance = (row - middle) / 0.6
    weight = jnp.exp(-0.5 * (distance * distance))
    return jnp.where((row >= cell) & (row < cell + KS), weight, F32(0.0))


def weight_rows(fine_index, cells):
    cell = jnp.floor(fine_index / OVER)
    tile = jnp.floor(cell / KS)
    inner = cell - tile * KS
    row = lax.broadcasted_iota(jnp.int32, (KS, fine_index.shape[1]), 0).astype(F32)
    wrapped = row < inner
    offset = row - inner + jnp.where(wrapped, F32(KS), F32(0.0))
    distance = (offset - ((KS - 1) / 2.0 + (fine_index / OVER - cell))) / 0.6
    weight = jnp.exp(-0.5 * (distance * distance))
    tile = tile + jnp.where(wrapped, F32(1.0), F32(0.0))
    return [jnp.where(tile == F32(n), weight, F32(0.0)) for n in range(cells // KS)]


def dot(left, right, dims):
    return lax.dot_general(left, right, (dims, ((), ())), preferred_element_type=F32)


def slot_rows(refs, slot):
    start = (slot % 2) * ROWS
    return refs[slot // 2], start


def slot_place(at, slot, groups):
    return ((at - (slot // 2) * 2) & (groups - 1)) ^ (slot % 2)


def lead_kernel(
    pos_ref, cnt_ref, y_hbm, u_hbm, v_hbm, obs_hbm, copy_hbm, meta_ref,
    u_ref, v_ref, obs_ref, load_sem, send_sem,
):
    slots = u_ref.shape[1]
    sends = [
        pltpu.make_async_copy(y_hbm, copy_hbm.at[n], send_sem.at[n])
        for n in range(copy_hbm.shape[0])
    ]
    for send in sends:
        send.start()
    pairs = [(u_hbm, u_ref), (v_hbm, v_ref), (obs_hbm, obs_ref)]
    loads = [
        pltpu.make_async_copy(source, target, load_sem.at[n])
        for n, (source, target) in enumerate(pairs)
    ]
    for load in loads:
        load.start()
    for load in loads:
        load.wait()
    meta_ref[0:1, :] = u_ref[...].astype(F32)
    meta_ref[1:2, :] = v_ref[...].astype(F32)
    meta_ref[2:3, :] = obs_ref[0]
    meta_ref[3:4, :] = obs_ref[1]
    meta_ref[4:5, :] = jnp.full((1, slots), pos_ref[0] // RES, jnp.int32).astype(F32)
    meta_ref[5:6, :] = jnp.full((1, slots), cnt_ref[0], jnp.int32).astype(F32)
    meta_ref[6:8, :] = jnp.zeros((2, slots), F32)
    for send in sends:
        send.wait()


def interleave(real, imag):
    parts = []
    for n in range(0, real.shape[1], RES):
        parts += [real[:, n : n + RES], imag[:, n : n + RES]]
    return jnp.concatenate(parts, 1)


def table_kernel(*refs):
    e_ref = refs[-1]
    pairs = refs[: len(refs) - 4]
    groups = 2 * len(pairs)
    spot = jnp.concatenate([p[n : n + 1, :] for p in pairs for n in (4, 4 + ROWS)], 0)
    step = jnp.concatenate([spot + F32(k) for k in range(KB)], 0).astype(jnp.int32)
    column = lax.broadcasted_iota(jnp.int32, step.shape, 1)
    turn = (step * column) & (SG - 1)
    angle = turn.astype(F32) * F32(2.0 * math.pi / SG)
    cos, sin = jnp.cos(angle) * F32(1.0 / 256.0), jnp.sin(angle) * F32(1.0 / 256.0)
    rows = []
    for k in range(KB):
        c, s = cos[k * groups : (k + 1) * groups], sin[k * groups : (k + 1) * groups]
        rows += [interleave(c, s), interleave(-s, c)]
    table = jnp.concatenate(rows, 0)
    high = table.astype(BF)
    e_ref[: table.shape[0], :] = high
    e_ref[table.shape[0] :, :] = (table - high.astype(F32)).astype(BF)


def slot_grid(ref, k, slot, groups, rows_v):
    real = ref[k, slot * rows_v : (slot + 1) * rows_v, :]
    imag = ref[k, (groups + slot) * rows_v : (groups + slot + 1) * rows_v, :]
    return jnp.concatenate([real, imag], 0)


def expand(wu_ref, fine_index):
    rows = weight_rows(fine_index, wu_ref.shape[0])
    for n in range(0, len(rows), 2):
        wu_ref[n * KS : (n + 2) * KS, :] = jnp.concatenate(rows[n : n + 2], 0).astype(BF)


def forward_kernel(y_ref, d_ref, tc_ref, ts_ref, e_ref, *refs):
    meta_refs = refs[:-4]
    part_ref, ys_ref, gs_ref, wu_ref = refs[-4:]
    groups = 2 * len(meta_refs)
    at = lax.axis_index("facet")
    d_table = d_ref[at]
    pieces = y_ref.shape[0]
    half = e_ref.shape[0] // 2
    band = half // KB
    rows_v = gs_ref.shape[1] // band
    lines = pieces // rows_v
    for k in range(KB):
        ys_ref[k] = y_ref[:, k * RES : (k + 1) * RES].astype(F32)
    for v in range(0, rows_v, BATCH):
        turned = []
        for n in range(BATCH):
            row = [ys_ref[k, pl.ds(v + n, lines, stride=rows_v), :] for k in range(KB)]
            row = jnp.concatenate(row, 1).astype(BF)
            spread = dot(d_table, jnp.concatenate([row, row], 0), ((1,), (0,)))
            spread = spread.reshape(RES // SUB, 2, SUB, SG)
            real_g, imag_g = spread[:, 0], spread[:, 1]
            cos = tc_ref[...].reshape(RES // SUB, SUB, SG)
            sin = ts_ref[...].reshape(RES // SUB, SUB, SG)
            real_h = (real_g * cos + imag_g * sin).reshape(RES, SG).astype(BF)
            imag_h = (imag_g * cos - real_g * sin).reshape(RES, SG).astype(BF)
            turned.append(interleave(real_h, imag_h))
        share = dot(e_ref[...], jnp.concatenate(turned, 0), ((1,), (1,)))
        share = share[:half] + share[half:]
        for n in range(BATCH):
            for k in range(KB):
                gs_ref[k, pl.ds(v + n, band, stride=rows_v), :] = share[
                    k * band : (k + 1) * band, n * RES : (n + 1) * RES
                ]
    for s in range(groups):
        grid = [slot_grid(gs_ref, k, s, groups, rows_v) for k in range(KB)]
        grid = jnp.concatenate(grid, 1)
        high = grid.astype(BF)
        low = (grid - high.astype(F32)).astype(BF)
        meta, start = slot_rows(meta_refs, s)
        expand(wu_ref.at[s], meta[start : start + 1, :])
        along = dot(jnp.concatenate([high, low], 0), wu_ref[s], ((1,), (0,)))
        along = along[: 2 * rows_v] + along[2 * rows_v :]
        wv = weights(meta[start + 1 : start + 2, :], rows_v)
        real = jnp.sum(along[:rows_v] * wv, 0, keepdims=True)
        imag = jnp.sum(along[rows_v:] * wv, 0, keepdims=True)
        place = slot_place(at, s, groups)
        both = jnp.concatenate([real, imag], 0).astype(BF)
        for n in range(groups):
            part_ref[n, place] = both


def backward_kernel(part_ref, e_ref, tc_ref, ts_ref, d_ref, *refs):
    meta_refs = refs[:-10]
    res_hbm, out_ref, pred_ref, rs_ref, im_ref, wu_ref, ct_ref, m_ref, res_ref, sem = refs[-10:]
    groups = 2 * len(meta_refs)
    slots = res_ref.shape[2]
    store = pltpu.make_async_copy(res_ref, res_hbm, sem)
    at = lax.axis_index("facet")
    d_table = d_ref[at]
    lines = d_table.shape[0]
    band = 2 * groups
    rows_v = rs_ref.shape[1] // band
    pred_ref[...] = jnp.sum(part_ref[...].astype(F32), 0)
    slot = lax.broadcasted_iota(jnp.int32, (2, slots), 1).astype(F32)
    for s in range(groups):
        place = slot_place(at, s, groups)
        meta, start = slot_rows(meta_refs, s)
        seen = meta[start + 2 : start + 4, :] - pred_ref[place]
        residual = jnp.where(slot < meta[start + 5 : start + 6, :], seen, F32(0.0))
        if s == 0:
            res_ref[0] = residual[0:1]
            res_ref[1] = residual[1:2]
            store.start()
        wv = weights(meta[start + 1 : start + 2, :], rows_v)
        spread = jnp.concatenate([wv * residual[0:1], wv * residual[1:2]], 0).astype(BF)
        expand(wu_ref.at[s], meta[start : start + 1, :])
        cells = dot(spread, wu_ref[s], ((1,), (1,)))
        for k in range(KB):
            part = cells[:, k * RES : (k + 1) * RES]
            rs_ref[k, s * rows_v : (s + 1) * rows_v, :] = part[:rows_v]
            rs_ref[k, (groups + s) * rows_v : (groups + s + 1) * rows_v, :] = part[rows_v:]
    for v in range(rows_v):
        rows = [rs_ref[k, pl.ds(v, band, stride=rows_v), :] for k in range(KB)]
        ct_ref[v] = jnp.concatenate(rows, 0).T.astype(BF)

    def turn_chunk(wave, f):
        v = wave * WAVE
        cells = ct_ref[v : v + WAVE, f : f + CHUNK, :].reshape(WAVE * CHUNK, KB * band)
        for n in range(0, SG, RES):
            cos = tc_ref[f : f + CHUNK, n : n + RES]
            sin = ts_ref[f : f + CHUNK, n : n + RES]
            back = dot(cells, e_ref[: KB * band, 2 * n : 2 * (n + RES)], ((1,), (0,)))
            back = back.reshape(WAVE, CHUNK, 2 * RES)
            real_b, imag_b = back[..., :RES], back[..., RES:]
            m_ref[v : v + WAVE, f : f + CHUNK, n : n + RES] = (
                real_b * cos - imag_b * sin
            ).astype(BF)
            m_ref[v : v + WAVE, RES + f : RES + f + CHUNK, n : n + RES] = (
                imag_b * cos + real_b * sin
            ).astype(BF)

    def make_block(v):
        image = dot(d_table, m_ref[v], ((1,), (0,)))
        for k in range(KB):
            im_ref[k, pl.ds(v, lines, stride=rows_v), :] = image[:, k * RES : (k + 1) * RES]

    waves = rows_v // WAVE
    steps = RES // CHUNK
    for wave in range(waves + 1):
        for n in range(steps):
            if wave < waves:
                turn_chunk(wave, n * CHUNK)
            if wave > 0:
                for v in range(n * WAVE // steps, (n + 1) * WAVE // steps):
                    make_block((wave - 1) * WAVE + v)
    for k in range(KB):
        out_ref[:, k * RES : (k + 1) * RES] = im_ref[k].astype(BF)
    store.wait()


def shards(facet_data, subgrid_pos, vis_counts, vis_u_fine, vis_v_fine, vis_observed):
    facets = lax.axis_size("facet")
    subs = lax.axis_size("sub")
    rows_v = facet_data.shape[1]
    slots = vis_u_fine.shape[1]

    params = pltpu.CompilerParams(vmem_limit_bytes=24 * 1024 * 1024)
    vmem = pl.BlockSpec(memory_space=pltpu.VMEM)
    hbm = pl.BlockSpec(memory_space=pltpu.HBM)
    smem = pl.BlockSpec(memory_space=pltpu.SMEM)
    copies, meta = pl.pallas_call(
        lead_kernel,
        out_shape=(
            jax.ShapeDtypeStruct((subs,) + facet_data.shape, BF),
            jax.ShapeDtypeStruct((ROWS, slots), F32),
        ),
        in_specs=[smem] * 2 + [hbm] * 4,
        out_specs=(hbm, vmem),
        scratch_shapes=[
            pltpu.VMEM((1, slots), jnp.int32),
            pltpu.VMEM((1, slots), jnp.int32),
            pltpu.VMEM((2, 1, slots), F32),
            pltpu.SemaphoreType.DMA((3,)),
            pltpu.SemaphoreType.DMA((subs,)),
        ],
        compiler_params=params,
        name="lead",
    )(
        subgrid_pos, vis_counts,
        *(
            pltpu.with_memory_space_constraint(value, pltpu.HBM)
            for value in (facet_data, vis_u_fine, vis_v_fine, vis_observed)
        ),
    )
    gathered = lax.all_to_all(copies, "sub", 0, 0, tiled=True)

    table = block_tables(facets, subs)
    high_d, low_d = host_split(table)
    into = np.concatenate([high_d, low_d], 2)
    into = into.reshape(facets, 2, RES // SUB, SUB, -1).swapaxes(1, 2)
    into = jnp.asarray(into.reshape(facets, 2 * RES, -1))
    outof = jnp.asarray(high_d.transpose(0, 2, 1))
    turn = np.arange(RES)[:, None] * np.arange(SG)[None, :] * (2.0 * math.pi / 65536)
    tw_cos = jnp.asarray(np.cos(turn).astype(np.float32))
    tw_sin = jnp.asarray(np.sin(turn).astype(np.float32))
    partner = lax.ppermute(meta, "facet", [(n, n ^ 1) for n in range(facets)])
    pairs = [jnp.concatenate([meta, partner], 0)]
    for d in range(2, facets, 2):
        ring = [(n, (n + d) % facets) for n in range(facets)]
        pairs.append(lax.ppermute(pairs[0], "facet", ring))

    e_table = pl.pallas_call(
        table_kernel,
        out_shape=jax.ShapeDtypeStruct((4 * KB * facets, 2 * SG), BF),
        in_specs=[vmem] * (3 + facets // 2),
        out_specs=vmem,
        compiler_params=params,
        name="position_table",
    )(*pairs, into, tw_cos, tw_sin)

    part = pl.pallas_call(
        forward_kernel,
        out_shape=jax.ShapeDtypeStruct((facets, facets, 2, slots), BF),
        in_specs=[vmem] * (5 + facets // 2),
        scratch_shapes=[
            pltpu.VMEM((KB, 2 * subs * rows_v, RES), F32),
            pltpu.VMEM((KB, 2 * facets * rows_v, RES), F32),
            pltpu.VMEM((facets, SG, slots), BF),
        ],
        compiler_params=params,
        name="forward_share",
    )(
        gathered.reshape(2 * subs * rows_v, SG), into, tw_cos, tw_sin, e_table,
        *pairs,
    )

    parts = lax.all_to_all(part, "facet", 0, 0, tiled=True)

    residual, image = pl.pallas_call(
        backward_kernel,
        out_shape=(
            jax.ShapeDtypeStruct((2, 1, slots), F32),
            jax.ShapeDtypeStruct((2 * subs * rows_v, SG), BF),
        ),
        in_specs=[vmem] * (5 + facets // 2),
        scratch_shapes=[
            pltpu.VMEM((facets, 2, slots), F32),
            pltpu.VMEM((KB, 2 * facets * rows_v, RES), F32),
            pltpu.VMEM((KB, 2 * subs * rows_v, RES), F32),
            pltpu.VMEM((facets, SG, slots), BF),
            pltpu.VMEM((rows_v, RES, 2 * KB * facets), BF),
            pltpu.VMEM((rows_v, 2 * RES, SG), BF),
            pltpu.VMEM((2, 1, slots), F32),
            pltpu.SemaphoreType.DMA(()),
        ],
        out_specs=(hbm, vmem),
        compiler_params=params,
        name="backward_share",
    )(parts, e_table, tw_cos, tw_sin, outof, *pairs)

    image = image.reshape(subs, 2, rows_v, SG)
    image = lax.all_to_all(image, "sub", 0, 0, tiled=True)
    return (residual, jnp.sum(image.astype(F32), 0))


def solution(mesh):
    return jax.shard_map(
        shards,
        mesh=mesh,
        in_specs=(
            P(None, None, ("facet", "sub")),
            P(("facet", "sub")),
            P(("facet", "sub")),
            P(("facet", "sub"), None),
            P(("facet", "sub"), None),
            P(None, ("facet", "sub"), None),
        ),
        out_specs=(P(None, ("facet", "sub"), None), P(None, None, ("facet", "sub"))),
        check_vma=False,
    )
```

```python
import math

import jax
import jax.numpy as jnp
import numpy as np
from jax import lax
from jax.experimental import pallas as pl
from jax.experimental.pallas import tpu as pltpu
from jax.sharding import PartitionSpec as P

SG = 512
KS = 8
OVER = 16
RES = 128
KB = SG // RES
BATCH = 4
CHUNK = 16
WAVE = 8
SUB = 8
ROWS = 8
BF = jnp.bfloat16
F32 = jnp.float32


def block_tables(facets, subs):
    block = np.arange(facets * subs).reshape(facets, subs)
    turn = (np.arange(RES)[None, :, None] * block[:, None, :]) % RES
    angle = turn * (2.0 * math.pi / RES)
    cos, sin = np.cos(angle), np.sin(angle)
    top = np.stack([cos, sin], -1)
    low = np.stack([-sin, cos], -1)
    table = np.concatenate([top, low], 1).reshape(facets, 2 * RES, 2 * subs)
    return table.astype(np.float32)


def host_split(table):
    high = table.astype(jnp.bfloat16)
    return high, (table - high.astype(np.float32)).astype(jnp.bfloat16)


def weights(fine_index, cells):
    middle = fine_index / OVER + (KS - 1) / 2.0
    cell = jnp.floor(fine_index / OVER)
    row = lax.broadcasted_iota(jnp.int32, (cells, fine_index.shape[1]), 0).astype(F32)
    distance = (row - middle) / 0.6
    weight = jnp.exp(-0.5 * (distance * distance))
    return jnp.where((row >= cell) & (row < cell + KS), weight, F32(0.0))


def weight_rows(fine_index, cells):
    cell = jnp.floor(fine_index / OVER)
    tile = jnp.floor(cell / KS)
    inner = cell - tile * KS
    row = lax.broadcasted_iota(jnp.int32, (KS, fine_index.shape[1]), 0).astype(F32)
    wrapped = row < inner
    offset = row - inner + jnp.where(wrapped, F32(KS), F32(0.0))
    distance = (offset - ((KS - 1) / 2.0 + (fine_index / OVER - cell))) / 0.6
    weight = jnp.exp(-0.5 * (distance * distance))
    tile = tile + jnp.where(wrapped, F32(1.0), F32(0.0))
    return [jnp.where(tile == F32(n), weight, F32(0.0)) for n in range(cells // KS)]


def dot(left, right, dims):
    return lax.dot_general(left, right, (dims, ((), ())), preferred_element_type=F32)


def slot_rows(refs, slot):
    start = (slot % 2) * ROWS
    return refs[slot // 2], start


def slot_place(at, slot, groups):
    return ((at - (slot // 2) * 2) & (groups - 1)) ^ (slot % 2)


def lead_kernel(
    pos_ref, cnt_ref, y_hbm, u_hbm, v_hbm, obs_hbm, copy_hbm, meta_ref,
    y_ref, many_ref, u_ref, v_ref, obs_ref, load_sem, send_sem,
):
    slots = u_ref.shape[1]
    pairs = [(y_hbm, y_ref), (u_hbm, u_ref), (v_hbm, v_ref), (obs_hbm, obs_ref)]
    loads = [
        pltpu.make_async_copy(source, target, load_sem.at[n])
        for n, (source, target) in enumerate(pairs)
    ]
    for load in loads:
        load.start()
    loads[0].wait()
    block = y_ref[...]
    repeats = many_ref.shape[0]
    for n in range(repeats):
        many_ref[n] = block
    sends = [
        pltpu.make_async_copy(
            many_ref, copy_hbm.at[pl.ds(n * repeats, repeats)], send_sem.at[n]
        )
        for n in range(copy_hbm.shape[0] // repeats)
    ]
    for send in sends:
        send.start()
    for load in loads[1:]:
        load.wait()
    meta_ref[0:1, :] = u_ref[...].astype(F32)
    meta_ref[1:2, :] = v_ref[...].astype(F32)
    meta_ref[2:3, :] = obs_ref[0]
    meta_ref[3:4, :] = obs_ref[1]
    meta_ref[4:5, :] = jnp.full((1, slots), pos_ref[0] // RES, jnp.int32).astype(F32)
    meta_ref[5:6, :] = jnp.full((1, slots), cnt_ref[0], jnp.int32).astype(F32)
    meta_ref[6:8, :] = jnp.zeros((2, slots), F32)
    for send in sends:
        send.wait()


def interleave(real, imag):
    parts = []
    for n in range(0, real.shape[1], RES):
        parts += [real[:, n : n + RES], imag[:, n : n + RES]]
    return jnp.concatenate(parts, 1)


def table_kernel(*refs):
    e_ref = refs[-1]
    pairs = refs[: len(refs) - 4]
    groups = 2 * len(pairs)
    spot = jnp.concatenate([p[n : n + 1, :] for p in pairs for n in (4, 4 + ROWS)], 0)
    step = jnp.concatenate([spot + F32(k) for k in range(KB)], 0).astype(jnp.int32)
    column = lax.broadcasted_iota(jnp.int32, step.shape, 1)
    turn = (step * column) & (SG - 1)
    angle = turn.astype(F32) * F32(2.0 * math.pi / SG)
    cos, sin = jnp.cos(angle) * F32(1.0 / 256.0), jnp.sin(angle) * F32(1.0 / 256.0)
    rows = []
    for k in range(KB):
        c, s = cos[k * groups : (k + 1) * groups], sin[k * groups : (k + 1) * groups]
        rows += [interleave(c, s), interleave(-s, c)]
    table = jnp.concatenate(rows, 0)
    high = table.astype(BF)
    e_ref[: table.shape[0], :] = high
    e_ref[table.shape[0] :, :] = (table - high.astype(F32)).astype(BF)


def slot_grid(ref, k, slot, groups, rows_v):
    real = ref[k, slot * rows_v : (slot + 1) * rows_v, :]
    imag = ref[k, (groups + slot) * rows_v : (groups + slot + 1) * rows_v, :]
    return jnp.concatenate([real, imag], 0)


def expand(wu_ref, fine_index):
    rows = weight_rows(fine_index, wu_ref.shape[0])
    for n in range(0, len(rows), 2):
        wu_ref[n * KS : (n + 2) * KS, :] = jnp.concatenate(rows[n : n + 2], 0).astype(BF)


def forward_kernel(y_ref, d_ref, tc_ref, ts_ref, e_ref, *refs):
    meta_refs = refs[:-4]
    part_ref, ys_ref, gs_ref, wu_ref = refs[-4:]
    groups = 2 * len(meta_refs)
    at = lax.axis_index("facet")
    d_table = d_ref[at]
    pieces = y_ref.shape[0]
    half = e_ref.shape[0] // 2
    band = half // KB
    rows_v = gs_ref.shape[1] // band
    lines = pieces // rows_v
    for k in range(KB):
        ys_ref[k] = y_ref[:, k * RES : (k + 1) * RES].astype(F32)
    for v in range(0, rows_v, BATCH):
        turned = []
        for n in range(BATCH):
            row = [ys_ref[k, pl.ds(v + n, lines, stride=rows_v), :] for k in range(KB)]
            row = jnp.concatenate(row, 1).astype(BF)
            spread = dot(d_table, jnp.concatenate([row, row], 0), ((1,), (0,)))
            spread = spread.reshape(RES // SUB, 2, SUB, SG)
            real_g, imag_g = spread[:, 0], spread[:, 1]
            cos = tc_ref[...].reshape(RES // SUB, SUB, SG)
            sin = ts_ref[...].reshape(RES // SUB, SUB, SG)
            real_h = (real_g * cos + imag_g * sin).reshape(RES, SG).astype(BF)
            imag_h = (imag_g * cos - real_g * sin).reshape(RES, SG).astype(BF)
            turned.append(interleave(real_h, imag_h))
        share = dot(e_ref[...], jnp.concatenate(turned, 0), ((1,), (1,)))
        share = share[:half] + share[half:]
        for n in range(BATCH):
            for k in range(KB):
                gs_ref[k, pl.ds(v + n, band, stride=rows_v), :] = share[
                    k * band : (k + 1) * band, n * RES : (n + 1) * RES
                ]
    for s in range(groups):
        grid = [slot_grid(gs_ref, k, s, groups, rows_v) for k in range(KB)]
        grid = jnp.concatenate(grid, 1)
        high = grid.astype(BF)
        low = (grid - high.astype(F32)).astype(BF)
        meta, start = slot_rows(meta_refs, s)
        expand(wu_ref.at[s], meta[start : start + 1, :])
        along = dot(jnp.concatenate([high, low], 0), wu_ref[s], ((1,), (0,)))
        along = along[: 2 * rows_v] + along[2 * rows_v :]
        wv = weights(meta[start + 1 : start + 2, :], rows_v)
        real = jnp.sum(along[:rows_v] * wv, 0, keepdims=True)
        imag = jnp.sum(along[rows_v:] * wv, 0, keepdims=True)
        place = slot_place(at, s, groups)
        both = jnp.concatenate([real, imag], 0).astype(BF)
        for n in range(groups):
            part_ref[n, place] = both


def backward_kernel(part_ref, e_ref, tc_ref, ts_ref, d_ref, *refs):
    meta_refs = refs[:-10]
    res_hbm, out_ref, pred_ref, rs_ref, im_ref, wu_ref, ct_ref, m_ref, res_ref, sem = refs[-10:]
    groups = 2 * len(meta_refs)
    slots = res_ref.shape[2]
    store = pltpu.make_async_copy(res_ref, res_hbm, sem)
    at = lax.axis_index("facet")
    d_table = d_ref[at]
    lines = d_table.shape[0]
    band = 2 * groups
    rows_v = rs_ref.shape[1] // band
    pred_ref[...] = jnp.sum(part_ref[...].astype(F32), 0)
    slot = lax.broadcasted_iota(jnp.int32, (2, slots), 1).astype(F32)
    for s in range(groups):
        place = slot_place(at, s, groups)
        meta, start = slot_rows(meta_refs, s)
        seen = meta[start + 2 : start + 4, :] - pred_ref[place]
        residual = jnp.where(slot < meta[start + 5 : start + 6, :], seen, F32(0.0))
        if s == 0:
            res_ref[0] = residual[0:1]
            res_ref[1] = residual[1:2]
            store.start()
        wv = weights(meta[start + 1 : start + 2, :], rows_v)
        spread = jnp.concatenate([wv * residual[0:1], wv * residual[1:2]], 0).astype(BF)
        expand(wu_ref.at[s], meta[start : start + 1, :])
        cells = dot(spread, wu_ref[s], ((1,), (1,)))
        for k in range(KB):
            part = cells[:, k * RES : (k + 1) * RES]
            rs_ref[k, s * rows_v : (s + 1) * rows_v, :] = part[:rows_v]
            rs_ref[k, (groups + s) * rows_v : (groups + s + 1) * rows_v, :] = part[rows_v:]
    for v in range(rows_v):
        rows = [rs_ref[k, pl.ds(v, band, stride=rows_v), :] for k in range(KB)]
        ct_ref[v] = jnp.concatenate(rows, 0).T.astype(BF)

    def turn_chunk(wave, f):
        v = wave * WAVE
        cells = ct_ref[v : v + WAVE, f : f + CHUNK, :].reshape(WAVE * CHUNK, KB * band)
        for n in range(0, SG, RES):
            cos = tc_ref[f : f + CHUNK, n : n + RES]
            sin = ts_ref[f : f + CHUNK, n : n + RES]
            back = dot(cells, e_ref[: KB * band, 2 * n : 2 * (n + RES)], ((1,), (0,)))
            back = back.reshape(WAVE, CHUNK, 2 * RES)
            real_b, imag_b = back[..., :RES], back[..., RES:]
            m_ref[v : v + WAVE, f : f + CHUNK, n : n + RES] = (
                real_b * cos - imag_b * sin
            ).astype(BF)
            m_ref[v : v + WAVE, RES + f : RES + f + CHUNK, n : n + RES] = (
                imag_b * cos + real_b * sin
            ).astype(BF)

    def make_block(v):
        image = dot(d_table, m_ref[v], ((1,), (0,)))
        for k in range(KB):
            im_ref[k, pl.ds(v, lines, stride=rows_v), :] = image[:, k * RES : (k + 1) * RES]

    waves = rows_v // WAVE
    steps = RES // CHUNK
    for wave in range(waves + 1):
        for n in range(steps):
            if wave < waves:
                turn_chunk(wave, n * CHUNK)
            if wave > 0:
                for v in range(n * WAVE // steps, (n + 1) * WAVE // steps):
                    make_block((wave - 1) * WAVE + v)
    for k in range(KB):
        out_ref[:, k * RES : (k + 1) * RES] = im_ref[k].astype(BF)
    store.wait()


def shards(facet_data, subgrid_pos, vis_counts, vis_u_fine, vis_v_fine, vis_observed):
    facets = lax.axis_size("facet")
    subs = lax.axis_size("sub")
    rows_v = facet_data.shape[1]
    slots = vis_u_fine.shape[1]

    params = pltpu.CompilerParams(vmem_limit_bytes=24 * 1024 * 1024)
    vmem = pl.BlockSpec(memory_space=pltpu.VMEM)
    hbm = pl.BlockSpec(memory_space=pltpu.HBM)
    smem = pl.BlockSpec(memory_space=pltpu.SMEM)
    copies, meta = pl.pallas_call(
        lead_kernel,
        out_shape=(
            jax.ShapeDtypeStruct((subs,) + facet_data.shape, BF),
            jax.ShapeDtypeStruct((ROWS, slots), F32),
        ),
        in_specs=[smem] * 2 + [hbm] * 4,
        out_specs=(hbm, vmem),
        scratch_shapes=[
            pltpu.VMEM(facet_data.shape, BF),
            pltpu.VMEM((subs // 2,) + facet_data.shape, BF),
            pltpu.VMEM((1, slots), jnp.int32),
            pltpu.VMEM((1, slots), jnp.int32),
            pltpu.VMEM((2, 1, slots), F32),
            pltpu.SemaphoreType.DMA((4,)),
            pltpu.SemaphoreType.DMA((2,)),
        ],
        compiler_params=params,
        name="lead",
    )(
        subgrid_pos, vis_counts,
        *(
            pltpu.with_memory_space_constraint(value, pltpu.HBM)
            for value in (facet_data, vis_u_fine, vis_v_fine, vis_observed)
        ),
    )
    gathered = lax.all_to_all(copies, "sub", 0, 0, tiled=True)

    table = block_tables(facets, subs)
    high_d, low_d = host_split(table)
    into = np.concatenate([high_d, low_d], 2)
    into = into.reshape(facets, 2, RES // SUB, SUB, -1).swapaxes(1, 2)
    into = jnp.asarray(into.reshape(facets, 2 * RES, -1))
    outof = jnp.asarray(high_d.transpose(0, 2, 1))
    turn = np.arange(RES)[:, None] * np.arange(SG)[None, :] * (2.0 * math.pi / 65536)
    tw_cos = jnp.asarray(np.cos(turn).astype(np.float32))
    tw_sin = jnp.asarray(np.sin(turn).astype(np.float32))
    partner = lax.ppermute(meta, "facet", [(n, n ^ 1) for n in range(facets)])
    pairs = [jnp.concatenate([meta, partner], 0)]
    for d in range(2, facets, 2):
        ring = [(n, (n + d) % facets) for n in range(facets)]
        pairs.append(lax.ppermute(pairs[0], "facet", ring))

    e_table = pl.pallas_call(
        table_kernel,
        out_shape=jax.ShapeDtypeStruct((4 * KB * facets, 2 * SG), BF),
        in_specs=[vmem] * (3 + facets // 2),
        out_specs=vmem,
        compiler_params=params,
        name="position_table",
    )(*pairs, into, tw_cos, tw_sin)

    part = pl.pallas_call(
        forward_kernel,
        out_shape=jax.ShapeDtypeStruct((facets, facets, 2, slots), BF),
        in_specs=[vmem] * (5 + facets // 2),
        scratch_shapes=[
            pltpu.VMEM((KB, 2 * subs * rows_v, RES), F32),
            pltpu.VMEM((KB, 2 * facets * rows_v, RES), F32),
            pltpu.VMEM((facets, SG, slots), BF),
        ],
        compiler_params=params,
        name="forward_share",
    )(
        gathered.reshape(2 * subs * rows_v, SG), into, tw_cos, tw_sin, e_table,
        *pairs,
    )

    parts = lax.all_to_all(part, "facet", 0, 0, tiled=True)

    residual, image = pl.pallas_call(
        backward_kernel,
        out_shape=(
            jax.ShapeDtypeStruct((2, 1, slots), F32),
            jax.ShapeDtypeStruct((2 * subs * rows_v, SG), BF),
        ),
        in_specs=[vmem] * (5 + facets // 2),
        scratch_shapes=[
            pltpu.VMEM((facets, 2, slots), F32),
            pltpu.VMEM((KB, 2 * facets * rows_v, RES), F32),
            pltpu.VMEM((KB, 2 * subs * rows_v, RES), F32),
            pltpu.VMEM((facets, SG, slots), BF),
            pltpu.VMEM((rows_v, RES, 2 * KB * facets), BF),
            pltpu.VMEM((rows_v, 2 * RES, SG), BF),
            pltpu.VMEM((2, 1, slots), F32),
            pltpu.SemaphoreType.DMA(()),
        ],
        out_specs=(hbm, vmem),
        compiler_params=params,
        name="backward_share",
    )(parts, e_table, tw_cos, tw_sin, outof, *pairs)

    image = image.reshape(subs, 2, rows_v, SG)
    image = lax.all_to_all(image, "sub", 0, 0, tiled=True)
    return (residual, jnp.sum(image.astype(F32), 0))


def solution(mesh):
    return jax.shard_map(
        shards,
        mesh=mesh,
        in_specs=(
            P(None, None, ("facet", "sub")),
            P(("facet", "sub")),
            P(("facet", "sub")),
            P(("facet", "sub"), None),
            P(("facet", "sub"), None),
            P(None, ("facet", "sub"), None),
        ),
        out_specs=(P(None, ("facet", "sub"), None), P(None, None, ("facet", "sub"))),
        check_vma=False,
    )
```

```python
import math

import jax
import jax.numpy as jnp
import numpy as np
from jax import lax
from jax.experimental import pallas as pl
from jax.experimental.pallas import tpu as pltpu
from jax.sharding import PartitionSpec as P

SG = 512
KS = 8
OVER = 16
RES = 128
KB = SG // RES
BATCH = 4
CHUNK = 16
WAVE = 8
SUB = 8
ROWS = 8
BF = jnp.bfloat16
F32 = jnp.float32


def block_tables(facets, subs):
    block = np.arange(facets * subs).reshape(facets, subs)
    turn = (np.arange(RES)[None, :, None] * block[:, None, :]) % RES
    angle = turn * (2.0 * math.pi / RES)
    cos, sin = np.cos(angle), np.sin(angle)
    top = np.stack([cos, sin], -1)
    low = np.stack([-sin, cos], -1)
    table = np.concatenate([top, low], 1).reshape(facets, 2 * RES, 2 * subs)
    return table.astype(np.float32)


def host_split(table):
    high = table.astype(jnp.bfloat16)
    return high, (table - high.astype(np.float32)).astype(jnp.bfloat16)


def weights(fine_index, cells):
    middle = fine_index / OVER + (KS - 1) / 2.0
    cell = jnp.floor(fine_index / OVER)
    row = lax.broadcasted_iota(jnp.int32, (cells, fine_index.shape[1]), 0).astype(F32)
    distance = (row - middle) / 0.6
    weight = jnp.exp(-0.5 * (distance * distance))
    return jnp.where((row >= cell) & (row < cell + KS), weight, F32(0.0))


def weight_rows(fine_index, cells):
    cell = jnp.floor(fine_index / OVER)
    tile = jnp.floor(cell / KS)
    inner = cell - tile * KS
    row = lax.broadcasted_iota(jnp.int32, (KS, fine_index.shape[1]), 0).astype(F32)
    wrapped = row < inner
    offset = row - inner + jnp.where(wrapped, F32(KS), F32(0.0))
    distance = (offset - ((KS - 1) / 2.0 + (fine_index / OVER - cell))) / 0.6
    weight = jnp.exp(-0.5 * (distance * distance))
    tile = tile + jnp.where(wrapped, F32(1.0), F32(0.0))
    return [jnp.where(tile == F32(n), weight, F32(0.0)) for n in range(cells // KS)]


def dot(left, right, dims):
    return lax.dot_general(left, right, (dims, ((), ())), preferred_element_type=F32)


def slot_rows(refs, slot):
    start = (slot % 2) * ROWS
    return refs[slot // 2], start


def slot_place(at, slot, groups):
    return ((at - (slot // 2) * 2) & (groups - 1)) ^ (slot % 2)


def lead_kernel(
    pos_ref, cnt_ref, y_hbm, u_hbm, v_hbm, obs_hbm, copy_hbm, meta_ref,
    y_ref, many_ref, u_ref, v_ref, obs_ref, load_sem, send_sem,
):
    slots = u_ref.shape[1]
    pairs = [(y_hbm, y_ref), (u_hbm, u_ref), (v_hbm, v_ref), (obs_hbm, obs_ref)]
    loads = [
        pltpu.make_async_copy(source, target, load_sem.at[n])
        for n, (source, target) in enumerate(pairs)
    ]
    for load in loads:
        load.start()
    loads[0].wait()
    block = y_ref[...]
    repeats = many_ref.shape[0]
    for n in range(repeats):
        many_ref[n] = block
    sends = [
        pltpu.make_async_copy(
            many_ref, copy_hbm.at[pl.ds(n * repeats, repeats)], send_sem.at[n]
        )
        for n in range(copy_hbm.shape[0] // repeats)
    ]
    for send in sends:
        send.start()
    for load in loads[1:]:
        load.wait()
    meta_ref[0:1, :] = u_ref[...].astype(F32)
    meta_ref[1:2, :] = v_ref[...].astype(F32)
    meta_ref[2:3, :] = obs_ref[0]
    meta_ref[3:4, :] = obs_ref[1]
    meta_ref[4:5, :] = jnp.full((1, slots), pos_ref[0] // RES, jnp.int32).astype(F32)
    meta_ref[5:6, :] = jnp.full((1, slots), cnt_ref[0], jnp.int32).astype(F32)
    meta_ref[6:8, :] = jnp.zeros((2, slots), F32)
    for send in sends:
        send.wait()


def interleave(real, imag):
    parts = []
    for n in range(0, real.shape[1], RES):
        parts += [real[:, n : n + RES], imag[:, n : n + RES]]
    return jnp.concatenate(parts, 1)


def table_kernel(*refs):
    e_ref = refs[-1]
    pairs = refs[: len(refs) - 4]
    groups = 2 * len(pairs)
    spot = jnp.concatenate([p[n : n + 1, :] for p in pairs for n in (4, 4 + ROWS)], 0)
    step = jnp.concatenate([spot + F32(k) for k in range(KB)], 0).astype(jnp.int32)
    column = lax.broadcasted_iota(jnp.int32, step.shape, 1)
    turn = (step * column) & (SG - 1)
    angle = turn.astype(F32) * F32(2.0 * math.pi / SG)
    cos, sin = jnp.cos(angle) * F32(1.0 / 256.0), jnp.sin(angle) * F32(1.0 / 256.0)
    rows = []
    for k in range(KB):
        c, s = cos[k * groups : (k + 1) * groups], sin[k * groups : (k + 1) * groups]
        rows += [interleave(c, s), interleave(-s, c)]
    table = jnp.concatenate(rows, 0)
    high = table.astype(BF)
    e_ref[: table.shape[0], :] = high
    e_ref[table.shape[0] :, :] = (table - high.astype(F32)).astype(BF)


def slot_grid(ref, k, slot, groups, rows_v):
    real = ref[k, slot * rows_v : (slot + 1) * rows_v, :]
    imag = ref[k, (groups + slot) * rows_v : (groups + slot + 1) * rows_v, :]
    return jnp.concatenate([real, imag], 0)


def expand(wu_ref, fine_index):
    rows = weight_rows(fine_index, wu_ref.shape[0])
    for n in range(0, len(rows), 2):
        wu_ref[n * KS : (n + 2) * KS, :] = jnp.concatenate(rows[n : n + 2], 0).astype(BF)


def forward_kernel(y_ref, d_ref, tc_ref, ts_ref, e_ref, *refs):
    meta_refs = refs[:-4]
    part_ref, ys_ref, gs_ref, wu_ref = refs[-4:]
    groups = 2 * len(meta_refs)
    at = lax.axis_index("facet")
    d_table = d_ref[at]
    pieces = y_ref.shape[0]
    half = e_ref.shape[0] // 2
    band = half // KB
    rows_v = gs_ref.shape[1] // band
    lines = pieces // rows_v
    for k in range(KB):
        ys_ref[k] = y_ref[:, k * RES : (k + 1) * RES].astype(F32)
    for v in range(0, rows_v, BATCH):
        turned = []
        for n in range(BATCH):
            row = [ys_ref[k, pl.ds(v + n, lines, stride=rows_v), :] for k in range(KB)]
            row = jnp.concatenate(row, 1).astype(BF)
            spread = dot(d_table, jnp.concatenate([row, row], 0), ((1,), (0,)))
            spread = spread.reshape(RES // SUB, 2, SUB, SG)
            real_g, imag_g = spread[:, 0], spread[:, 1]
            cos = tc_ref[...].reshape(RES // SUB, SUB, SG)
            sin = ts_ref[...].reshape(RES // SUB, SUB, SG)
            real_h = (real_g * cos + imag_g * sin).reshape(RES, SG).astype(BF)
            imag_h = (imag_g * cos - real_g * sin).reshape(RES, SG).astype(BF)
            turned.append(interleave(real_h, imag_h))
        share = dot(e_ref[...], jnp.concatenate(turned, 0), ((1,), (1,)))
        share = share[:half] + share[half:]
        for n in range(BATCH):
            for k in range(KB):
                gs_ref[k, pl.ds(v + n, band, stride=rows_v), :] = share[
                    k * band : (k + 1) * band, n * RES : (n + 1) * RES
                ]
    for s in range(groups):
        grid = [slot_grid(gs_ref, k, s, groups, rows_v) for k in range(KB)]
        grid = jnp.concatenate(grid, 1)
        high = grid.astype(BF)
        low = (grid - high.astype(F32)).astype(BF)
        meta, start = slot_rows(meta_refs, s)
        expand(wu_ref.at[s], meta[start : start + 1, :])
        along = dot(jnp.concatenate([high, low], 0), wu_ref[s], ((1,), (0,)))
        along = along[: 2 * rows_v] + along[2 * rows_v :]
        wv = weights(meta[start + 1 : start + 2, :], rows_v)
        real = jnp.sum(along[:rows_v] * wv, 0, keepdims=True)
        imag = jnp.sum(along[rows_v:] * wv, 0, keepdims=True)
        place = slot_place(at, s, groups)
        both = jnp.concatenate([real, imag], 0).astype(BF)
        for n in range(groups):
            part_ref[n, place] = both


def backward_kernel(part_ref, e_ref, tc_ref, ts_ref, d_ref, *refs):
    meta_refs = refs[:-10]
    res_hbm, out_ref, pred_ref, rs_ref, im_ref, wu_ref, ct_ref, m_ref, res_ref, sem = refs[-10:]
    groups = 2 * len(meta_refs)
    slots = res_ref.shape[2]
    store = pltpu.make_async_copy(res_ref, res_hbm, sem)
    at = lax.axis_index("facet")
    d_table = d_ref[at]
    lines = d_table.shape[0]
    band = 2 * groups
    rows_v = rs_ref.shape[1] // band
    pred_ref[...] = jnp.sum(part_ref[...].astype(F32), 0)
    slot = lax.broadcasted_iota(jnp.int32, (2, slots), 1).astype(F32)
    for s in range(groups):
        place = slot_place(at, s, groups)
        meta, start = slot_rows(meta_refs, s)
        seen = meta[start + 2 : start + 4, :] - pred_ref[place]
        residual = jnp.where(slot < meta[start + 5 : start + 6, :], seen, F32(0.0))
        if s == 0:
            res_ref[0] = residual[0:1]
            res_ref[1] = residual[1:2]
            store.start()
        wv = weights(meta[start + 1 : start + 2, :], rows_v)
        spread = jnp.concatenate([wv * residual[0:1], wv * residual[1:2]], 0).astype(BF)
        expand(wu_ref.at[s], meta[start : start + 1, :])
        cells = dot(spread, wu_ref[s], ((1,), (1,)))
        for k in range(KB):
            part = cells[:, k * RES : (k + 1) * RES]
            rs_ref[k, s * rows_v : (s + 1) * rows_v, :] = part[:rows_v]
            rs_ref[k, (groups + s) * rows_v : (groups + s + 1) * rows_v, :] = part[rows_v:]
    for v in range(rows_v):
        rows = [rs_ref[k, pl.ds(v, band, stride=rows_v), :] for k in range(KB)]
        ct_ref[v] = jnp.concatenate(rows, 0).T.astype(BF)

    def turn_chunk(wave, f):
        v = wave * WAVE
        cells = ct_ref[v : v + WAVE, f : f + CHUNK, :].reshape(WAVE * CHUNK, KB * band)
        for n in range(0, SG, RES):
            cos = tc_ref[f : f + CHUNK, n : n + RES].astype(BF)
            sin = ts_ref[f : f + CHUNK, n : n + RES].astype(BF)
            back = dot(cells, e_ref[: KB * band, 2 * n : 2 * (n + RES)], ((1,), (0,)))
            back = back.reshape(WAVE, CHUNK, 2 * RES).astype(BF)
            real_b, imag_b = back[..., :RES], back[..., RES:]
            m_ref[v : v + WAVE, f : f + CHUNK, n : n + RES] = real_b * cos - imag_b * sin
            m_ref[v : v + WAVE, RES + f : RES + f + CHUNK, n : n + RES] = (
                imag_b * cos + real_b * sin
            )

    def make_block(v):
        image = dot(d_table, m_ref[v], ((1,), (0,)))
        for k in range(KB):
            im_ref[k, pl.ds(v, lines, stride=rows_v), :] = image[:, k * RES : (k + 1) * RES]

    waves = rows_v // WAVE
    steps = RES // CHUNK
    for wave in range(waves + 1):
        for n in range(steps):
            if wave < waves:
                turn_chunk(wave, n * CHUNK)
            if wave > 0:
                for v in range(n * WAVE // steps, (n + 1) * WAVE // steps):
                    make_block((wave - 1) * WAVE + v)
    for k in range(KB):
        out_ref[:, k * RES : (k + 1) * RES] = im_ref[k].astype(BF)
    store.wait()


def shards(facet_data, subgrid_pos, vis_counts, vis_u_fine, vis_v_fine, vis_observed):
    facets = lax.axis_size("facet")
    subs = lax.axis_size("sub")
    rows_v = facet_data.shape[1]
    slots = vis_u_fine.shape[1]

    params = pltpu.CompilerParams(vmem_limit_bytes=24 * 1024 * 1024)
    vmem = pl.BlockSpec(memory_space=pltpu.VMEM)
    hbm = pl.BlockSpec(memory_space=pltpu.HBM)
    smem = pl.BlockSpec(memory_space=pltpu.SMEM)
    copies, meta = pl.pallas_call(
        lead_kernel,
        out_shape=(
            jax.ShapeDtypeStruct((subs,) + facet_data.shape, BF),
            jax.ShapeDtypeStruct((ROWS, slots), F32),
        ),
        in_specs=[smem] * 2 + [hbm] * 4,
        out_specs=(hbm, vmem),
        scratch_shapes=[
            pltpu.VMEM(facet_data.shape, BF),
            pltpu.VMEM((subs // 2,) + facet_data.shape, BF),
            pltpu.VMEM((1, slots), jnp.int32),
            pltpu.VMEM((1, slots), jnp.int32),
            pltpu.VMEM((2, 1, slots), F32),
            pltpu.SemaphoreType.DMA((4,)),
            pltpu.SemaphoreType.DMA((2,)),
        ],
        compiler_params=params,
        name="lead",
    )(
        subgrid_pos, vis_counts,
        *(
            pltpu.with_memory_space_constraint(value, pltpu.HBM)
            for value in (facet_data, vis_u_fine, vis_v_fine, vis_observed)
        ),
    )
    gathered = lax.all_to_all(copies, "sub", 0, 0, tiled=True)

    table = block_tables(facets, subs)
    high_d, low_d = host_split(table)
    into = np.concatenate([high_d, low_d], 2)
    into = into.reshape(facets, 2, RES // SUB, SUB, -1).swapaxes(1, 2)
    into = jnp.asarray(into.reshape(facets, 2 * RES, -1))
    outof = jnp.asarray(high_d.transpose(0, 2, 1))
    turn = np.arange(RES)[:, None] * np.arange(SG)[None, :] * (2.0 * math.pi / 65536)
    tw_cos = jnp.asarray(np.cos(turn).astype(np.float32))
    tw_sin = jnp.asarray(np.sin(turn).astype(np.float32))
    partner = lax.ppermute(meta, "facet", [(n, n ^ 1) for n in range(facets)])
    pairs = [jnp.concatenate([meta, partner], 0)]
    for d in range(2, facets, 2):
        ring = [(n, (n + d) % facets) for n in range(facets)]
        pairs.append(lax.ppermute(pairs[0], "facet", ring))

    e_table = pl.pallas_call(
        table_kernel,
        out_shape=jax.ShapeDtypeStruct((4 * KB * facets, 2 * SG), BF),
        in_specs=[vmem] * (3 + facets // 2),
        out_specs=vmem,
        compiler_params=params,
        name="position_table",
    )(*pairs, into, tw_cos, tw_sin)

    part = pl.pallas_call(
        forward_kernel,
        out_shape=jax.ShapeDtypeStruct((facets, facets, 2, slots), BF),
        in_specs=[vmem] * (5 + facets // 2),
        scratch_shapes=[
            pltpu.VMEM((KB, 2 * subs * rows_v, RES), F32),
            pltpu.VMEM((KB, 2 * facets * rows_v, RES), F32),
            pltpu.VMEM((facets, SG, slots), BF),
        ],
        compiler_params=params,
        name="forward_share",
    )(
        gathered.reshape(2 * subs * rows_v, SG), into, tw_cos, tw_sin, e_table,
        *pairs,
    )

    parts = lax.all_to_all(part, "facet", 0, 0, tiled=True)

    residual, image = pl.pallas_call(
        backward_kernel,
        out_shape=(
            jax.ShapeDtypeStruct((2, 1, slots), F32),
            jax.ShapeDtypeStruct((2 * subs * rows_v, SG), BF),
        ),
        in_specs=[vmem] * (5 + facets // 2),
        scratch_shapes=[
            pltpu.VMEM((facets, 2, slots), F32),
            pltpu.VMEM((KB, 2 * facets * rows_v, RES), F32),
            pltpu.VMEM((KB, 2 * subs * rows_v, RES), F32),
            pltpu.VMEM((facets, SG, slots), BF),
            pltpu.VMEM((rows_v, RES, 2 * KB * facets), BF),
            pltpu.VMEM((rows_v, 2 * RES, SG), BF),
            pltpu.VMEM((2, 1, slots), F32),
            pltpu.SemaphoreType.DMA(()),
        ],
        out_specs=(hbm, vmem),
        compiler_params=params,
        name="backward_share",
    )(parts, e_table, tw_cos, tw_sin, outof, *pairs)

    image = image.reshape(subs, 2, rows_v, SG)
    image = lax.all_to_all(image, "sub", 0, 0, tiled=True)
    return (residual, jnp.sum(image.astype(F32), 0))


def solution(mesh):
    return jax.shard_map(
        shards,
        mesh=mesh,
        in_specs=(
            P(None, None, ("facet", "sub")),
            P(("facet", "sub")),
            P(("facet", "sub")),
            P(("facet", "sub"), None),
            P(("facet", "sub"), None),
            P(None, ("facet", "sub"), None),
        ),
        out_specs=(P(None, ("facet", "sub"), None), P(None, None, ("facet", "sub"))),
        check_vma=False,
    )
```
